512 devices in a mesh: row: 32 (over x_hi, z, core), col: 16 (over y, x_lo).
Axes of the slice: x: 4 (x_hi: 2, x_lo: 2; x = x_hi * 2 + x_lo), y: 8, z: 8, core: 2. Of those that a mesh axis runs over, the one named last changes fastest.
Arguments:
- pre_silu: bfloat16 [8, 96, 96, 256], P(None, 'row', 'col'), may hold values from -6 to 6
- out_grad: bfloat16 [8, 96, 96, 256], P(None, 'row', 'col'), may hold values from -6 to 6
- query_heads: bfloat16 [32, 9216, 64], P('col', 'row'), may hold values from -10 to 10
- key_heads: bfloat16 [32, 9216, 64], P('col', 'row'), may hold values from -10 to 10
- value_heads: bfloat16 [32, 9216, 64], P('col', 'row'), may hold values from -6 to 6
- conv_weight: bfloat16 [3, 3, 256, 256], replicated, may hold values from -0.125 to 0.125
- out_weight: bfloat16 [256, 256], replicated, may hold values from -0.375 to 0.375
- input_weight: bfloat16 [256, 768], replicated, may hold values from -0.375 to 0.375
Outputs:
- grad_input: bfloat16 [8, 96, 96, 256], P(None, 'row', 'col')
The draws below stay inside these ranges and needn't reach their ends.
All inputs are finite; a program needn't handle non-finite values.
Results may differ from the reference program's by a relative error of at most 0.0095.
Values may be sent and summed in bfloat16 or wider, within the bound.
A program may use at most 64 MiB of HBM per device.

```python
import jax
import jax.numpy as jnp
from jax import lax

C = 256
HEADS = 4
HD = 64
TR = 3
SAMPLES = 8
HGT = 96
WID = 96
TOKENS = 9216
COMBOS = 32
N_ROW = 32


def drawn_pair(key):
    folded = jax.random.fold_in(key, 4242)
    key_one, key_two = jax.random.split(folded, 2)
    full_shape = (COMBOS, TOKENS, HD)
    queries = jnp.clip(1.4 * jax.random.normal(key_one, full_shape), -8.0, 8.0)
    keys_all = jnp.clip(1.4 * jax.random.normal(key_two, full_shape), -8.0, 8.0)
    return (queries, keys_all)


def draw_query_heads(key, part):
    return drawn_pair(key)[0].astype(jnp.bfloat16)


def draw_key_heads(key, part):
    return drawn_pair(key)[1].astype(jnp.bfloat16)


def steps_of(key, extent, cuts, smallest, top_value):
    def one(position, blocks):
        steps = jax.random.uniform(jax.random.fold_in(jax.random.fold_in(key, 6), position), (blocks,), jnp.float32, smallest / len(cuts), top_value / len(cuts))
        return jnp.repeat(jnp.exp(steps), extent[position] // blocks).reshape((-1,) + (1,) * (len(extent) - position - 1))

    loudness = one(*cuts[0])
    for cut in cuts[1:]:
        loudness = loudness * one(*cut)
    return loudness


def centred(rng, extent, scale, reach, cuts=(), kind=jnp.bfloat16):
    result = jax.random.normal(rng, extent, jnp.float32) * scale
    if len(cuts) > 0:
        result = steps_of(rng, extent, cuts, -0.22, 0.18) * result
    return jnp.clip(result, min=-reach, max=reach).astype(kind)


def setup_inputs(seed: int = 0) -> dict:
    splits = jax.random.split(jax.random.key(seed), 9)
    return {
        "pre_silu": centred(splits[0], (SAMPLES, HGT, WID, C), 1.5, 6.0, ((1, 32), (2, 16))),
        "out_grad": centred(splits[1], (SAMPLES, HGT, WID, C), 1.0, 6.0, ((1, 32), (2, 16))),
        "query_heads": draw_query_heads(jax.random.fold_in(splits[8], 71), 0),
        "key_heads": draw_key_heads(jax.random.fold_in(splits[8], 71), 0),
        "value_heads": centred(splits[4], (COMBOS, TOKENS, HD), 1.0, 6.0, ((0, 16), (1, 32))),
        "conv_weight": centred(splits[5], (3, 3, C, C), (9 * C) ** -0.5, 0.125),
        "out_weight": centred(splits[6], (C, C), C ** -0.5, 0.375),
        "input_weight": centred(splits[7], (C, 3 * C), C ** -0.5, 0.375),
    }


def reference(pre_silu, out_grad, query_heads, key_heads, value_heads, conv_weight, out_weight, input_weight):
    factor = HD ** -0.5
    padded = jnp.pad(out_grad.astype(jnp.float32), ((0, 0), (1, 1), (1, 1), (0, 0)))
    kernel = conv_weight.astype(jnp.float32)
    conv_sum = jnp.zeros((SAMPLES, HGT, WID, C), jnp.float32)
    for shift_r in (-1, 0, 1):
        for shift_c in (-1, 0, 1):
            window = padded[:, 1 - shift_r:1 - shift_r + HGT, 1 - shift_c:1 - shift_c + WID, :]
            conv_sum = conv_sum + jnp.einsum('srcd,ed->srce', window, kernel[shift_r + 1, shift_c + 1])
    z_float = pre_silu.astype(jnp.float32)
    sigmoid_z = jax.nn.sigmoid(z_float)
    grad_z = (conv_sum * sigmoid_z * (1.0 + z_float * (1.0 - sigmoid_z))).astype(jnp.bfloat16)
    grad_attn = jnp.einsum('srcd,hed->shrce', grad_z.astype(jnp.float32),
                           out_weight.astype(jnp.float32).reshape(HEADS, HD, C)).astype(jnp.bfloat16)
    grad_attn = grad_attn.reshape(COMBOS, TOKENS, HD)
    strip_rows = TR * WID

    def one_combo(operands):
        queries, keys_all, values, grad_out = operands

        def strip_step(running, pieces):
            grad_key, grad_value = running
            query_strip, grad_strip = pieces
            scores = jnp.dot(query_strip, keys_all.T, preferred_element_type=jnp.float32) * factor
            log_norm = jax.scipy.special.logsumexp(scores, axis=1)
            prob_block = jnp.exp(scores - log_norm[:, None])
            grad_probs = jnp.dot(grad_strip, values.T, preferred_element_type=jnp.float32)
            row_dot = jnp.sum(prob_block * grad_probs, axis=1)
            grad_scores = (prob_block * (grad_probs - row_dot[:, None])).astype(jnp.bfloat16)
            grad_query = jnp.dot(grad_scores, keys_all, preferred_element_type=jnp.float32) * factor
            grad_key = grad_key + jnp.dot(grad_scores.T, query_strip, preferred_element_type=jnp.float32) * factor
            grad_value = grad_value + jnp.dot(prob_block.astype(jnp.bfloat16).T, grad_strip,
                                              preferred_element_type=jnp.float32)
            return (grad_key, grad_value), grad_query

        zero_rows = jnp.zeros((TOKENS, HD), jnp.float32)
        finals, grad_query = lax.scan(strip_step, (zero_rows, zero_rows),
                                      (queries.reshape(N_ROW, strip_rows, HD), grad_out.reshape(N_ROW, strip_rows, HD)))
        return jnp.stack([grad_query.reshape(TOKENS, HD), finals[0], finals[1]]).astype(jnp.bfloat16)

    grads = lax.map(one_combo, (query_heads, key_heads, value_heads, grad_attn))
    stacked = grads.reshape(SAMPLES, HEADS, 3, HGT, WID, HD).astype(jnp.float32)
    projected = jnp.einsum('shkrce,dkhe->srcd', stacked, input_weight.astype(jnp.float32).reshape(C, 3, HEADS, HD))
    return (grad_z.astype(jnp.float32) + projected).astype(jnp.bfloat16)
```

```python
import functools

import jax
import jax.numpy as jnp
import numpy as np
from jax import lax
from jax.experimental import pallas as pl
from jax.experimental.pallas import tpu as pltpu
from jax.sharding import PartitionSpec as P

BF = jnp.bfloat16
F32 = jnp.float32
SAMPLES, HEADS, HD, C = 8, 4, 64, 256
TR, TC = 3, 6
N_ROW, N_COL = 32, 16
WID = TC * N_COL
STRIP = TR * WID
HALF = STRIP // 2
BLOCK = 8 * STRIP
CHUNK = 256
CHUNKS = BLOCK // CHUNK
PAD = 32
TILE = TR * TC
MESH = pl.DeviceIdType.MESH
FACTOR = HD**-0.5
KAPPA = FACTOR * float(np.log2(np.e))
NT = (((1,), (1,)), ((), ()))


def selections():
    tile = np.zeros((SAMPLES * PAD, TILE * SAMPLES), np.float32)
    for s in range(SAMPLES):
        for t in range(TILE):
            tile[s * PAD + t, t * SAMPLES + s] = 1.0
    strip = np.zeros((STRIP, N_COL * PAD), np.float32)
    for row in range(TR):
        for col in range(WID):
            strip[row * WID + col, (col // TC) * PAD + row * TC + col % TC] = 1.0
    return tile, strip, strip.T


def dot(a, b):
    return jnp.dot(a, b, preferred_element_type=F32)


def dot_nt(a, b):
    return lax.dot_general(a, b, NT, preferred_element_type=F32)


def swap(x):
    return pltpu.roll(x, 64, 1)


def kernel(
    og, zz, qh, kh, vh, cw, ow, iw, sel_tile, sel_strip, sel_back,
    out,
    xp, gz_keep, ga_s, do_r, qpk, opk, kvpk, q_r, o_r, kv_r, qz, oz, do_t, k_t, v_t1,
    o_t, st_s, st_r, kvo, kv_part, dq_t, qo, q_part, g_s, g_r,
    halo_send, halo_recv, a_send, a_recv, q_send, q_recv, o_send, o_recv,
    k_send, k_recv, t_send, t_recv, p_send, p_recv, d_send, d_recv, b_send, b_recv,
):
    r = lax.axis_index("row")
    c = lax.axis_index("col")
    core = lax.rem(r, 2)
    other = 1 - core
    zi = lax.rem(r // 2, 8)
    xh = r // 16
    zl = lax.rem(zi, 2)
    nq = xh * 2 + zl
    nk = zi // 2

    def q_base(n):
        return (n // 2) * 16 + (2 * nk + lax.rem(n, 2)) * 2

    def k_base(n):
        return xh * 16 + (2 * n + zl) * 2

    def wrap(x, n):
        return lax.rem(x + n, n)

    lanes = lax.broadcasted_iota(jnp.int32, (HALF, 128), 1) < 64
    lanes_strip = lax.broadcasted_iota(jnp.int32, (STRIP, 128), 1) < 64
    lanes_chunk = lax.broadcasted_iota(jnp.int32, (CHUNK, 128), 1) < 64

    barrier = pltpu.get_barrier_semaphore()
    shifts = [(i, j) for i in (-1, 0, 1) for j in (-1, 0, 1) if (i, j) != (0, 0)]
    peers = [(wrap(r + i, N_ROW), wrap(c + j, N_COL)) for i, j in shifts]
    peers += [(r, lax.rem(c + o, N_COL)) for o in range(2, N_COL - 1)]
    for base, own in ((q_base, nq), (k_base, nk)):
        for o in range(1, 4):
            n = lax.rem(own + o, 4)
            peers += [(base(n), c), (base(n) + 1, c)]
    peers += [(r + 1 - 2 * core, c)]
    for peer in peers:
        pl.semaphore_signal(barrier, inc=1, device_id=peer, device_id_type=MESH)

    for p in range(2):
        qpk[p] = jnp.concatenate([qh[p, :HALF, :], qh[p, HALF:, :]], axis=1)
        kvpk[p] = jnp.concatenate([kh[p], vh[p]], axis=1)
    xp[1:4, 1:7] = og[...]
    pl.semaphore_wait(barrier, len(peers))

    def push(src, dst, send, recv, peer):
        copy = pltpu.make_async_remote_copy(
            src_ref=src, dst_ref=dst, send_sem=send, recv_sem=recv,
            device_id=peer, device_id_type=MESH,
        )
        return copy

    def rim(shift, width, take):
        if shift == 0:
            return pl.ds(0, width) if take else pl.ds(1, width)
        if take:
            return pl.ds(width - 1, 1) if shift == 1 else pl.ds(0, 1)
        return pl.ds(0, 1) if shift == 1 else pl.ds(width + 1, 1)

    halos = []
    for index, (i, j) in enumerate(shifts):
        halos.append(
            push(
                og.at[rim(i, TR, True), rim(j, TC, True)],
                xp.at[rim(i, TR, False), rim(j, TC, False)],
                halo_send.at[index], halo_recv.at[index],
                (wrap(r + i, N_ROW), wrap(c + j, N_COL)),
            )
        )
    for copy in halos:
        copy.start()

    def gather(src, dst, base, own, send, recv):
        slot = own * 2 + core
        started, arrivals = [], []
        dst[slot] = src[core]
        started.append(
            push(src.at[other], dst.at[slot], send.at[0], recv.at[0], (r + 1 - 2 * core, c))
        )
        arrivals.append(
            push(src.at[0], dst.at[own * 2 + other], send.at[0], recv.at[0],
                 (r + 1 - 2 * core, c))
        )
        for o in range(1, 4):
            n = lax.rem(own + o, 4)
            back = lax.rem(own + 4 - o, 4)
            for p in range(2):
                place = 1 + (o - 1) * 2
                started.append(
                    push(src.at[p], dst.at[slot], send.at[place + p], recv.at[place + core],
                         (base(n) + p, c))
                )
                arrivals.append(
                    push(src.at[p], dst.at[back * 2 + p], send.at[place + p],
                         recv.at[place + p], (base(back) + p, c))
                )
        for copy in started:
            copy.start()
        return started, arrivals

    kv_out, kv_in = gather(kvpk, kv_r, k_base, nk, k_send, k_recv)
    q_out, q_in = gather(qpk, q_r, q_base, nq, q_send, q_recv)

    for copy in halos:
        copy.wait_recv()
    zero_row = jnp.zeros((1, TC + 2, SAMPLES, C), BF)
    zero_col = jnp.zeros((TR + 2, 1, SAMPLES, C), BF)

    @pl.when(r == 0)
    def _():
        xp[0:1] = zero_row

    @pl.when(r == N_ROW - 1)
    def _():
        xp[TR + 1 : TR + 2] = zero_row

    @pl.when(c == 0)
    def _():
        xp[:, 0:1] = zero_col

    @pl.when(c == N_COL - 1)
    def _():
        xp[:, TC + 1 : TC + 2] = zero_col

    cells = xp[...].astype(F32)
    conv = jnp.zeros((TILE * SAMPLES, C), F32)
    for a in (-1, 0, 1):
        for b in (-1, 0, 1):
            window = cells[1 - a : 1 - a + TR, 1 - b : 1 - b + TC]
            window = window.reshape(TILE * SAMPLES, C).astype(BF)
            conv = conv + dot_nt(window, cw[a + 1, b + 1])
    z = zz[...].astype(F32).reshape(TILE * SAMPLES, C)
    sig = jax.nn.sigmoid(z)
    grad_z = (conv * sig * (1.0 + z * (1.0 - sig))).astype(BF)
    placed = dot(sel_tile[...], grad_z)
    gz_keep[...] = placed
    ga = dot_nt(placed.astype(BF), ow[...]).astype(BF)
    for s in range(SAMPLES):
        for b in range(2):
            ga_s[2 * s + b] = ga[s * PAD : (s + 1) * PAD, b * 128 : (b + 1) * 128]

    def exchange(src, dst, send, recv):
        dst[c] = src[c]
        started, arrivals = [], []
        for o in range(1, N_COL):
            to, back = lax.rem(c + o, N_COL), lax.rem(c + N_COL - o, N_COL)
            started.append(push(src.at[to], dst.at[c], send.at[o], recv.at[o], (r, to)))
            arrivals.append(push(src.at[back], dst.at[back], send.at[o], recv.at[o], (r, back)))
        for copy in started:
            copy.start()
        return started, arrivals

    a_out, a_in = exchange(ga_s, do_r, a_send, a_recv)
    for copy in a_in:
        copy.wait_recv()
    strip = dot(sel_strip[...], do_r[...].reshape(N_COL * PAD, 128))
    top, bottom = strip[:HALF], strip[HALF:]
    opk[0] = jnp.where(lanes, top, swap(bottom)).astype(BF)
    opk[1] = jnp.where(lanes, swap(top), bottom).astype(BF)
    o_out, o_in = gather(opk, o_r, q_base, nq, o_send, o_recv)

    for copy in q_in + kv_in:
        copy.wait_recv()
    for k in range(8):
        x = q_r[k].astype(F32)
        qz[k * STRIP : k * STRIP + HALF] = jnp.where(lanes, x, 0.0).astype(BF)
        qz[k * STRIP + HALF : (k + 1) * STRIP] = jnp.where(lanes, swap(x), 0.0).astype(BF)
    keys = kv_r.reshape(BLOCK, 128)
    v_t1[:, 64:80, :] = jnp.ones((CHUNKS, 16, CHUNK), BF)
    for k in range(CHUNKS):
        turned = keys[k * CHUNK : (k + 1) * CHUNK].astype(F32).T.astype(BF)
        k_t[k] = turned[:64]
        v_t1[k, 0:64, :] = turned[64:]

    def stats_step(j, carry):
        at = pl.multiple_of(j * CHUNK, CHUNK)
        scores = dot_nt(keys[...], qz[pl.ds(at, CHUNK)])
        top = jnp.max(scores, axis=0, keepdims=True) * KAPPA
        e = jnp.exp2(scores * KAPPA - top)
        st_s[0:1, pl.ds(at, CHUNK)] = top
        st_s[1:2, pl.ds(at, CHUNK)] = jnp.sum(e, axis=0, keepdims=True)
        eb = e.astype(BF)
        acc = jnp.zeros((80, CHUNK), F32)
        for k in range(CHUNKS):
            acc = acc + dot(v_t1[k], eb[k * CHUNK : (k + 1) * CHUNK])
        st_s[2:3, pl.ds(at, CHUNK)] = acc[64:65]
        o_t[:, pl.ds(at, CHUNK)] = acc[:64]
        return carry

    lax.fori_loop(0, CHUNKS, stats_step, 0)

    for copy in o_in:
        copy.wait_recv()
    for k in range(8):
        x = o_r[k].astype(F32)
        oz[k * STRIP : k * STRIP + HALF] = jnp.where(lanes, 0.0, swap(x)).astype(BF)
        oz[k * STRIP + HALF : (k + 1) * STRIP] = jnp.where(lanes, 0.0, x).astype(BF)
    for k in range(CHUNKS):
        at = slice(k * CHUNK, (k + 1) * CHUNK)
        do_t[:, at] = oz[at].astype(F32).T[64:]
    st_s[3:4] = jnp.sum(o_t[...] * do_t[...], axis=0, keepdims=True)

    st_r[nq] = st_s[...]
    t_out, t_in = [], []
    for o in range(1, 4):
        n, back = lax.rem(nq + o, 4), lax.rem(nq + 4 - o, 4)
        t_out.append(push(st_s, st_r.at[nq], t_send.at[o], t_recv.at[o], (q_base(n) + core, c)))
        t_in.append(
            push(st_s, st_r.at[back], t_send.at[o], t_recv.at[o], (q_base(back) + core, c))
        )
    for copy in t_out:
        copy.start()
    for copy in t_in:
        copy.wait_recv()
    tops = [st_r[n, 0:1] for n in range(4)]
    top = jnp.maximum(jnp.maximum(tops[0], tops[1]), jnp.maximum(tops[2], tops[3]))
    norm = norm_b = weighted = jnp.zeros((1, BLOCK), F32)
    for n in range(4):
        scale = jnp.exp2(tops[n] - top)
        norm = norm + scale * st_r[n, 1:2]
        norm_b = norm_b + scale * st_r[n, 2:3]
        weighted = weighted + scale * st_r[n, 3:4]
    log_norm = top + jnp.log(norm) * float(np.log2(np.e))
    row_dot = weighted / norm_b

    dq_t[...] = jnp.zeros_like(dq_t)
    mine = nk * 2 + core

    def part_copy(k):
        at = pl.multiple_of(k * STRIP, 32)
        return push(
            kvo.at[pl.ds(at, STRIP)], kv_part.at[core, nk], p_send.at[k],
            p_recv.at[core, nk], (k_base(k // 2) + lax.rem(k, 2), c),
        )

    def grad_step(j, carry):
        at = pl.multiple_of(j * CHUNK, CHUNK)
        kv = keys[pl.ds(at, CHUNK)]
        probs = jnp.exp2(dot_nt(kv, qz[...]) * KAPPA - log_norm)
        grad_probs = dot_nt(kv, oz[...])
        grad_scores = (probs * (grad_probs - row_dot)).astype(BF)
        both = dot(grad_scores, qz[...]) + dot(probs.astype(BF), oz[...])
        kvo[pl.ds(at, CHUNK)] = jnp.where(lanes_chunk, both * FACTOR, both).astype(BF)
        dq_t[0:64] += dot(k_t[j], grad_scores)
        k = j - 1

        @pl.when(jnp.logical_and(k >= 0, k != mine))
        def _():
            part_copy(k).start()

        return carry

    lax.fori_loop(0, CHUNKS, grad_step, 0)
    kv_part[core, nk] = kvo[pl.ds(pl.multiple_of(mine * STRIP, 32), STRIP)]

    turned = dq_t[...].T * FACTOR
    for k in range(8):
        first = turned[k * STRIP : k * STRIP + HALF]
        second = turned[k * STRIP + HALF : (k + 1) * STRIP]
        qo[k] = (first + swap(second)).astype(BF)
    mine_q = nq * 2 + core
    q_part[core, nq] = qo[mine_q]

    def dq_copy(k):
        return push(
            qo.at[k], q_part.at[core, nq], d_send.at[k], d_recv.at[core, nq],
            (q_base(k // 2) + k % 2, c),
        )

    for k in range(8):

        @pl.when(k != mine_q)
        def _():
            dq_copy(k).start()

    def arrive(dst, recv, base, own, src):
        for p in range(2):
            for n in range(4):

                @pl.when(jnp.logical_or(n != own, p != core))
                def _():
                    push(src, dst.at[p, n], d_send.at[0], recv.at[p, n],
                         (base(n) + p, c)).wait_recv()

    arrive(kv_part, p_recv, k_base, nk, kvo.at[pl.ds(0, STRIP)])
    arrive(q_part, d_recv, q_base, nq, qo.at[0])
    kv0, kv1 = [
        kv_part[p, 0].astype(F32) + kv_part[p, 1].astype(F32)
        + kv_part[p, 2].astype(F32) + kv_part[p, 3].astype(F32)
        for p in range(2)
    ]
    q0, q1 = [
        q_part[p, 0].astype(F32) + q_part[p, 1].astype(F32)
        + q_part[p, 2].astype(F32) + q_part[p, 3].astype(F32)
        for p in range(2)
    ]
    dq_top = jnp.where(lanes, q0, swap(q1))
    dq_bottom = jnp.where(lanes, swap(q0), q1)
    dk = jnp.where(lanes_strip, kv0, swap(kv1)).astype(BF)
    dv = jnp.where(lanes_strip, swap(kv0), kv1).astype(BF)
    back = sel_back[...]
    placed_q = (
        dot(back[:, :HALF], dq_top.astype(BF)) + dot(back[:, HALF:], dq_bottom.astype(BF))
    )
    for kind, placed in enumerate((placed_q, dot(back, dk), dot(back, dv))):
        placed = placed.astype(BF)
        for n in range(N_COL):
            g_s[n, :, kind * 128 : (kind + 1) * 128] = placed[n * PAD : (n + 1) * PAD]
    b_out, b_in = exchange(g_s, g_r, b_send, b_recv)
    for copy in b_in:
        copy.wait_recv()

    total = gz_keep[...]
    for b in range(2):
        got = jnp.concatenate([g_r[2 * s + b] for s in range(SAMPLES)], axis=0)
        for kind in range(3):
            weight = iw[:, kind * 256 + b * 128 : kind * 256 + (b + 1) * 128]
            total = total + dot_nt(got[:, kind * 128 : (kind + 1) * 128], weight)
    out[...] = total.astype(BF)

    for copy in halos + kv_out + q_out + a_out + o_out + t_out + b_out:
        copy.wait_send()
    for k in range(8):

        @pl.when(k != mine)
        def _():
            part_copy(k).wait_send()

        @pl.when(k != mine_q)
        def _():
            dq_copy(k).wait_send()


def shards(
    pre_silu, out_grad, query_heads, key_heads, value_heads, conv_weight, out_weight, input_weight
):
    sel_tile, sel_strip, sel_back = [jnp.asarray(x, BF) for x in selections()]
    og = jnp.transpose(out_grad, (1, 2, 0, 3))
    zz = jnp.transpose(pre_silu, (1, 2, 0, 3))
    vmem = pl.BlockSpec(memory_space=pltpu.VMEM)
    dma = lambda *n: pltpu.SemaphoreType.DMA(n)
    result = pl.pallas_call(
        kernel,
        out_shape=jax.ShapeDtypeStruct((SAMPLES * PAD, C), BF),
        in_specs=[vmem] * 11,
        out_specs=vmem,
        scratch_shapes=[
            pltpu.VMEM((TR + 2, TC + 2, SAMPLES, C), BF),
            pltpu.VMEM((SAMPLES * PAD, C), F32),
            pltpu.VMEM((N_COL, PAD, 128), BF),
            pltpu.VMEM((N_COL, PAD, 128), BF),
            pltpu.VMEM((2, HALF, 128), BF),
            pltpu.VMEM((2, HALF, 128), BF),
            pltpu.VMEM((2, STRIP, 128), BF),
            pltpu.VMEM((8, HALF, 128), BF),
            pltpu.VMEM((8, HALF, 128), BF),
            pltpu.VMEM((8, STRIP, 128), BF),
            pltpu.VMEM((BLOCK, 128), BF),
            pltpu.VMEM((BLOCK, 128), BF),
            pltpu.VMEM((64, BLOCK), F32),
            pltpu.VMEM((CHUNKS, 64, CHUNK), BF),
            pltpu.VMEM((CHUNKS, 80, CHUNK), BF),
            pltpu.VMEM((64, BLOCK), F32),
            pltpu.VMEM((4, BLOCK), F32),
            pltpu.VMEM((4, 4, BLOCK), F32),
            pltpu.VMEM((BLOCK, 128), BF),
            pltpu.VMEM((2, 4, STRIP, 128), BF),
            pltpu.VMEM((128, BLOCK), F32),
            pltpu.VMEM((8, HALF, 128), BF),
            pltpu.VMEM((2, 4, HALF, 128), BF),
            pltpu.VMEM((N_COL, PAD, 384), BF),
            pltpu.VMEM((N_COL, PAD, 384), BF),
            dma(8), dma(8), dma(16), dma(16), dma(7), dma(7), dma(7), dma(7),
            dma(7), dma(7), dma(4), dma(4), dma(8), dma(2, 4), dma(8), dma(2, 4),
            dma(16), dma(16),
        ],
        compiler_params=pltpu.CompilerParams(
            collective_id=0, has_side_effects=True, vmem_limit_bytes=56 * 2**20
        ),
    )(
        og, zz, query_heads, key_heads, value_heads, conv_weight, out_weight, input_weight,
        sel_tile, sel_strip, sel_back,
    )
    result = result.reshape(SAMPLES, PAD, C)[:, :TILE]
    return result.reshape(SAMPLES, TR, TC, C)


def solution(mesh):
    in_specs = (
        P(None, "row", "col", None),
        P(None, "row", "col", None),
        P("col", "row", None),
        P("col", "row", None),
        P("col", "row", None),
        P(),
        P(),
        P(),
    )
    out_specs = P(None, "row", "col", None)
    return jax.shard_map(shards, mesh=mesh, in_specs=in_specs, out_specs=out_specs, check_vma=False)
```

```python
import functools

import jax
import jax.numpy as jnp
import numpy as np
from jax import lax
from jax.experimental import pallas as pl
from jax.experimental.pallas import tpu as pltpu
from jax.sharding import PartitionSpec as P

BF = jnp.bfloat16
F32 = jnp.float32
SAMPLES, HEADS, HD, C = 8, 4, 64, 256
TR, TC = 3, 6
N_ROW, N_COL = 32, 16
WID = TC * N_COL
STRIP = TR * WID
HALF = STRIP // 2
BLOCK = 8 * STRIP
CHUNK = 256
CHUNKS = BLOCK // CHUNK
PAD = 32
TILE = TR * TC
MESH = pl.DeviceIdType.MESH
FACTOR = HD**-0.5
KAPPA = FACTOR * float(np.log2(np.e))
NT = (((1,), (1,)), ((), ()))


REST = STRIP - CHUNK
MSG = 48


def spot(half, token):
    return half * 16 + token if token < 16 else 32 + half * 2 + token - 16


def selections():
    tile = np.zeros((SAMPLES * PAD, TILE * SAMPLES), np.float32)
    strip = np.zeros((STRIP, N_COL * PAD), np.float32)
    back = np.zeros((N_COL * MSG, 2 * STRIP), np.float32)
    got = np.zeros((2 * TILE * SAMPLES, N_COL * MSG), np.float32)
    for t in range(TILE):
        for s in range(SAMPLES):
            tile[s * PAD + t, t * SAMPLES + s] = 1.0
        for n in range(N_COL):
            place = (t // TC) * WID + n * TC + t % TC
            strip[place, n * PAD + t] = 1.0
            for half in range(2):
                back[n * MSG + spot(half, t), half * STRIP + place] = 1.0
                row = half * TILE * SAMPLES + t * SAMPLES + n // 2
                got[row, n * MSG + spot(half, t)] = 1.0
    return tile, strip, back, got


def dot(a, b):
    return jnp.dot(a, b, preferred_element_type=F32)


def dot_nt(a, b):
    return lax.dot_general(a, b, NT, preferred_element_type=F32)


def swap(x):
    return pltpu.roll(x, 64, 1)


def kernel(
    og, zz, qh, kh, vh, cw, ow, iw, sel_tile, sel_strip, sel_back, sel_got,
    out,
    xp, gz_keep, ga_s, do_r, qpk, opk, kvpk, q_r, o_r, kv_r, qz, oz, do_t, k_t, v_t1,
    o_t, st_s, st_r, kvo, kv_part, dq_t, qo, q_part, g_s, g_r,
    halo_send, halo_recv, a_send, a_recv, q_send, q_recv, o_send, o_recv,
    k_send, k_recv, t_send, t_recv, p_send, p_recv, d_send, d_recv, b_send, b_recv,
):
    r = lax.axis_index("row")
    c = lax.axis_index("col")
    core = lax.rem(r, 2)
    other = 1 - core
    zi = lax.rem(r // 2, 8)
    xh = r // 16
    zl = lax.rem(zi, 2)
    mq = zi // 2

    def q_peer(o):
        return xh * 16 + (2 * lax.rem(mq + o, 4) + zl) * 2

    def k_peer(o):
        return lax.rem(xh + o // 2, 2) * 16 + (2 * mq + lax.rem(zl + lax.rem(o, 2), 2)) * 2

    def wrap(x, n):
        return lax.rem(x + n, n)

    lanes = lax.broadcasted_iota(jnp.int32, (HALF, 128), 1) < 64
    lanes_strip = lax.broadcasted_iota(jnp.int32, (STRIP, 128), 1) < 64
    lanes_chunk = lax.broadcasted_iota(jnp.int32, (CHUNK, 128), 1) < 64

    barrier = pltpu.get_barrier_semaphore()
    shifts = [(i, j) for i in (-1, 0, 1) for j in (-1, 0, 1) if (i, j) != (0, 0)]
    peers = [(wrap(r + i, N_ROW), wrap(c + j, N_COL)) for i, j in shifts]
    peers += [(r, lax.rem(c + o, N_COL)) for o in range(2, N_COL - 1)]
    for peer in (q_peer, k_peer):
        for o in range(1, 4):
            peers += [(peer(o), c), (peer(o) + 1, c)]
    peers += [(r + 1 - 2 * core, c)]
    for peer in peers:
        pl.semaphore_signal(barrier, inc=1, device_id=peer, device_id_type=MESH)

    def halves(x, dst):
        top, bottom = x[:HALF], x[HALF:]
        dst[0] = jnp.where(lanes, top, swap(bottom)).astype(BF)
        dst[1] = jnp.where(lanes, swap(top), bottom).astype(BF)

    for p in range(2):
        kvpk[p] = jnp.concatenate([kh[p], vh[p]], axis=0).T
    halves(jnp.concatenate([qh[0], qh[1]], axis=0).T.astype(F32), qpk)
    xp[1:4, 1:7] = og[...]
    pl.semaphore_wait(barrier, len(peers))

    def push(src, dst, send, recv, peer):
        copy = pltpu.make_async_remote_copy(
            src_ref=src, dst_ref=dst, send_sem=send, recv_sem=recv,
            device_id=peer, device_id_type=MESH,
        )
        return copy

    def rim(shift, width, take):
        if shift == 0:
            return pl.ds(0, width) if take else pl.ds(1, width)
        if take:
            return pl.ds(width - 1, 1) if shift == 1 else pl.ds(0, 1)
        return pl.ds(0, 1) if shift == 1 else pl.ds(width + 1, 1)

    halos = []
    for index, (i, j) in enumerate(shifts):
        halos.append(
            push(
                og.at[rim(i, TR, True), rim(j, TC, True)],
                xp.at[rim(i, TR, False), rim(j, TC, False)],
                halo_send.at[index], halo_recv.at[index],
                (wrap(r + i, N_ROW), wrap(c + j, N_COL)),
            )
        )
    for copy in halos:
        copy.start()

    def gather(src, dst, peer, slot, turn, order, send, recv):
        here = (r + 1 - 2 * core, c)
        dst[slot(0) * 2 + core] = src[core]
        started = [
            push(src.at[other], dst.at[slot(0) * 2 + core], send.at[0], recv.at[0], here)
        ]
        arrivals = {
            0: [push(src.at[0], dst.at[slot(0) * 2 + other], send.at[0], recv.at[0], here)]
        }
        for o in order:
            there = turn(o)
            arrivals[o] = []
            for p in range(2):
                started.append(
                    push(src.at[p], dst.at[slot(o, True) * 2 + core], send.at[2 * o + p],
                         recv.at[2 * there + core], (peer(o) + p, c))
                )
                arrivals[o].append(
                    push(src.at[p], dst.at[slot(o) * 2 + p], send.at[2 * o + p],
                         recv.at[2 * o + p], (peer(o) + p, c))
                )
        for copy in started:
            copy.start()
        return started, arrivals

    def k_slot(o, remote=False):
        return 3 - o

    def q_slot(o, remote=False):
        return mq if remote else lax.rem(mq + o, 4)

    ring = lambda o: (4 - o) % 4
    kv_out, kv_in = gather(kvpk, kv_r, k_peer, k_slot, lambda o: o, (1, 2, 3), k_send, k_recv)
    q_out, q_in = gather(qpk, q_r, q_peer, q_slot, ring, (1, 3, 2), q_send, q_recv)

    for copy in halos:
        copy.wait_recv()
    zero_row = jnp.zeros((1, TC + 2, SAMPLES, C), BF)
    zero_col = jnp.zeros((TR + 2, 1, SAMPLES, C), BF)

    @pl.when(r == 0)
    def _():
        xp[0:1] = zero_row

    @pl.when(r == N_ROW - 1)
    def _():
        xp[TR + 1 : TR + 2] = zero_row

    @pl.when(c == 0)
    def _():
        xp[:, 0:1] = zero_col

    @pl.when(c == N_COL - 1)
    def _():
        xp[:, TC + 1 : TC + 2] = zero_col

    cells = xp[...].astype(F32)
    conv = jnp.zeros((TILE * SAMPLES, C), F32)
    for a in (-1, 0, 1):
        for b in (-1, 0, 1):
            window = cells[1 - a : 1 - a + TR, 1 - b : 1 - b + TC]
            window = window.reshape(TILE * SAMPLES, C).astype(BF)
            conv = conv + dot_nt(window, cw[a + 1, b + 1])
    z = zz[...].astype(F32).reshape(TILE * SAMPLES, C)
    sig = jax.nn.sigmoid(z)
    grad_z = (conv * sig * (1.0 + z * (1.0 - sig))).astype(BF)
    gz_keep[...] = grad_z.astype(F32)
    placed = dot(sel_tile[...], grad_z)
    ga = dot_nt(placed.astype(BF), ow[...]).astype(BF)
    for s in range(SAMPLES):
        for b in range(2):
            ga_s[2 * s + b] = ga[s * PAD : (s + 1) * PAD, b * 128 : (b + 1) * 128]

    def exchange(src, dst, send, recv):
        dst[c] = src[c]
        started, arrivals = [], []
        for o in range(1, N_COL):
            to, back = lax.rem(c + o, N_COL), lax.rem(c + N_COL - o, N_COL)
            started.append(push(src.at[to], dst.at[c], send.at[o], recv.at[o], (r, to)))
            arrivals.append(
                push(src.at[back], dst.at[back], send.at[o], recv.at[o], (r, back))
            )
        for copy in started:
            copy.start()
        return started, arrivals

    a_out, a_in = exchange(ga_s, do_r, a_send, a_recv)

    def unpack(src, slot, dst, left):
        x = src[slot].astype(F32)
        if left:
            top, bottom = jnp.where(lanes, x, 0.0), jnp.where(lanes, swap(x), 0.0)
        else:
            top, bottom = jnp.where(lanes, 0.0, swap(x)), jnp.where(lanes, 0.0, x)
        bottom = bottom.astype(BF)
        at = pl.multiple_of(slot * CHUNK, CHUNK)
        dst[pl.ds(at, HALF)] = top.astype(BF)
        dst[pl.ds(at + HALF, CHUNK - HALF)] = bottom[: CHUNK - HALF]
        rest = pl.multiple_of(8 * CHUNK + slot * REST, REST)
        dst[pl.ds(rest, REST)] = bottom[CHUNK - HALF :]

    for o in range(4):
        for copy in kv_in[o]:
            copy.wait_recv()
    keys = kv_r.reshape(BLOCK, 128)
    v_t1[:, 64:80, :] = jnp.ones((CHUNKS, 16, CHUNK), BF)
    for k in range(CHUNKS):
        turned = keys[k * CHUNK : (k + 1) * CHUNK].astype(F32).T.astype(BF)
        k_t[k] = turned[:64]
        v_t1[k, 0:64, :] = turned[64:]

    def stats_chunk(at):
        scores = dot_nt(keys[...], qz[pl.ds(at, CHUNK)])
        top = jnp.max(scores, axis=0, keepdims=True) * KAPPA
        e = jnp.exp2(scores * KAPPA - top)
        st_s[0:1, pl.ds(at, CHUNK)] = top
        st_s[1:2, pl.ds(at, CHUNK)] = jnp.sum(e, axis=0, keepdims=True)
        eb = e.astype(BF)
        acc = jnp.zeros((80, CHUNK), F32)
        for k in range(CHUNKS):
            acc = acc + dot(v_t1[k], eb[k * CHUNK : (k + 1) * CHUNK])
        st_s[2:3, pl.ds(at, CHUNK)] = acc[64:65]
        o_t[:, pl.ds(at, CHUNK)] = acc[:64]

    def stats_member(o):
        for copy in q_in[o]:
            copy.wait_recv()

        def step(k, carry):
            slot = q_slot(o) * 2 + k
            unpack(q_r, slot, qz, True)
            stats_chunk(pl.multiple_of(slot * CHUNK, CHUNK))
            return carry

        lax.fori_loop(0, 2, step, 0)

    stats_member(0)
    for copy in a_in:
        copy.wait_recv()
    halves(dot(sel_strip[...], do_r[...].reshape(N_COL * PAD, 128)), opk)
    o_out, o_in = gather(opk, o_r, q_peer, q_slot, ring, (1, 3, 2), o_send, o_recv)
    for o in (1, 3, 2):
        stats_member(o)
    stats_chunk(8 * CHUNK)

    for o in range(4):
        for copy in o_in[o]:
            copy.wait_recv()
    for k in range(8):
        unpack(o_r, k, oz, False)
    for k in range(CHUNKS):
        at = slice(k * CHUNK, (k + 1) * CHUNK)
        do_t[:, at] = oz[at].astype(F32).T[64:]
    st_s[3:4] = jnp.sum(o_t[...] * do_t[...], axis=0, keepdims=True)

    st_r[0] = st_s[...]
    t_out, t_in = [], []
    for o in range(1, 4):
        peer = (q_peer(o) + core, c)
        t_out.append(push(st_s, st_r.at[ring(o)], t_send.at[o], t_recv.at[ring(o)], peer))
        t_in.append(push(st_s, st_r.at[o], t_send.at[o], t_recv.at[o], peer))
    for copy in t_out:
        copy.start()
    for copy in t_in:
        copy.wait_recv()
    tops = [st_r[n, 0:1] for n in range(4)]
    top = jnp.maximum(jnp.maximum(tops[0], tops[1]), jnp.maximum(tops[2], tops[3]))
    norm = norm_b = weighted = jnp.zeros((1, BLOCK), F32)
    for n in range(4):
        scale = jnp.exp2(tops[n] - top)
        norm = norm + scale * st_r[n, 1:2]
        norm_b = norm_b + scale * st_r[n, 2:3]
        weighted = weighted + scale * st_r[n, 3:4]
    log_norm = top + jnp.log(norm) * float(np.log2(np.e))
    row_dot = weighted / norm_b

    dq_t[...] = jnp.zeros_like(dq_t)
    mine = 6 + core

    def part_copy(k):
        at = pl.multiple_of(k * STRIP, 32)
        o = 3 - k // 2
        return push(
            kvo.at[pl.ds(at, STRIP)], kv_part.at[core, o], p_send.at[k],
            p_recv.at[core, o], (k_peer(o) + lax.rem(k, 2), c),
        )

    def grad_step(j, carry):
        at = pl.multiple_of(j * CHUNK, CHUNK)
        kv = keys[pl.ds(at, CHUNK)]
        probs = jnp.exp2(dot_nt(kv, qz[...]) * KAPPA - log_norm)
        grad_probs = dot_nt(kv, oz[...])
        grad_scores = (probs * (grad_probs - row_dot)).astype(BF)
        both = dot(grad_scores, qz[...]) + dot(probs.astype(BF), oz[...])
        kvo[pl.ds(at, CHUNK)] = jnp.where(lanes_chunk, both * FACTOR, both).astype(BF)
        dq_t[0:64] += dot(k_t[j], grad_scores)
        k = j - 1

        @pl.when(jnp.logical_and(k >= 0, k != mine))
        def _():
            part_copy(k).start()

        return carry

    lax.fori_loop(0, CHUNKS, grad_step, 0)
    kv_part[core, 0] = kvo[pl.ds(pl.multiple_of(mine * STRIP, 32), STRIP)]

    turned = dq_t[...].T * FACTOR
    for k in range(8):
        main = turned[k * CHUNK : (k + 1) * CHUNK]
        rest = turned[8 * CHUNK + k * REST : 8 * CHUNK + (k + 1) * REST]
        second = jnp.concatenate([main[HALF:], rest], axis=0)
        qo[k] = (main[:HALF] + swap(second)).astype(BF)
    q_part[core, 0] = qo[mq * 2 + core]
    d_out = [
        push(qo.at[q_slot(o) * 2 + p], q_part.at[core, ring(o)], d_send.at[2 * o + p],
             d_recv.at[core, ring(o)], (q_peer(o) + p, c))
        for o in (2, 1, 3) for p in range(2)
    ]
    d_out.append(
        push(qo.at[mq * 2 + other], q_part.at[core, 0], d_send.at[0], d_recv.at[core, 0],
             (r + 1 - 2 * core, c))
    )
    for copy in d_out:
        copy.start()

    def arrive(src, dst, send, recv, peer):
        push(src, dst.at[other, 0], send.at[0], recv.at[other, 0],
             (r + 1 - 2 * core, c)).wait_recv()
        for o in range(1, 4):
            for p in range(2):
                push(src, dst.at[p, o], send.at[0], recv.at[p, o], (peer(o) + p, c)).wait_recv()

    arrive(kvo.at[pl.ds(0, STRIP)], kv_part, p_send, p_recv, k_peer)
    arrive(qo.at[0], q_part, d_send, d_recv, q_peer)
    kv0, kv1 = [
        kv_part[p, 0].astype(F32) + kv_part[p, 1].astype(F32)
        + kv_part[p, 2].astype(F32) + kv_part[p, 3].astype(F32)
        for p in range(2)
    ]
    q0, q1 = [
        q_part[p, 0].astype(F32) + q_part[p, 1].astype(F32)
        + q_part[p, 2].astype(F32) + q_part[p, 3].astype(F32)
        for p in range(2)
    ]
    dq_top = jnp.where(lanes, q0, swap(q1))
    dq_bottom = jnp.where(lanes, swap(q0), q1)
    dk = jnp.where(lanes_strip, kv0, swap(kv1)).astype(BF)
    dv = jnp.where(lanes_strip, swap(kv0), kv1).astype(BF)
    dq = jnp.concatenate([dq_top, dq_bottom], axis=0).astype(BF)

    projected = jnp.zeros((STRIP, C), F32)
    for kind, grad in enumerate((dq, dk, dv)):
        at = pl.multiple_of(kind * C + lax.rem(c, 2) * 128, 128)
        projected = projected + dot_nt(grad, iw[:, pl.ds(at, 128)])
    projected = projected.astype(BF)
    projected = jnp.concatenate([projected[:, :128], projected[:, 128:]], axis=0)
    g_s[...] = dot(sel_back[...], projected).astype(BF).reshape(N_COL, MSG, 128)
    b_out, b_in = exchange(g_s, g_r, b_send, b_recv)
    for copy in b_in:
        copy.wait_recv()
    sums = dot(sel_got[...], g_r[...].reshape(N_COL * MSG, 128))
    rows = TILE * SAMPLES
    total = gz_keep[...] + jnp.concatenate([sums[:rows], sums[rows:]], axis=1)
    out[...] = total.astype(BF)

    for copy in halos + kv_out + q_out + a_out + o_out + t_out + b_out:
        copy.wait_send()
    for copy in d_out:
        copy.wait_send()
    for k in range(8):

        @pl.when(k != mine)
        def _():
            part_copy(k).wait_send()


def shards(
    pre_silu, out_grad, query_heads, key_heads, value_heads, conv_weight, out_weight, input_weight
):
    sel = [jnp.asarray(x, BF) for x in selections()]
    turn = lambda x: jnp.transpose(x, (0, 2, 1))
    og = jnp.transpose(out_grad, (1, 2, 0, 3))
    zz = jnp.transpose(pre_silu, (1, 2, 0, 3))
    vmem = pl.BlockSpec(memory_space=pltpu.VMEM)
    dma = lambda *n: pltpu.SemaphoreType.DMA(n)
    result = pl.pallas_call(
        kernel,
        out_shape=jax.ShapeDtypeStruct((TILE * SAMPLES, C), BF),
        in_specs=[vmem] * 12,
        out_specs=vmem,
        scratch_shapes=[
            pltpu.VMEM((TR + 2, TC + 2, SAMPLES, C), BF),
            pltpu.VMEM((TILE * SAMPLES, C), F32),
            pltpu.VMEM((N_COL, PAD, 128), BF),
            pltpu.VMEM((N_COL, PAD, 128), BF),
            pltpu.VMEM((2, HALF, 128), BF),
            pltpu.VMEM((2, HALF, 128), BF),
            pltpu.VMEM((2, STRIP, 128), BF),
            pltpu.VMEM((8, HALF, 128), BF),
            pltpu.VMEM((8, HALF, 128), BF),
            pltpu.VMEM((8, STRIP, 128), BF),
            pltpu.VMEM((BLOCK, 128), BF),
            pltpu.VMEM((BLOCK, 128), BF),
            pltpu.VMEM((64, BLOCK), F32),
            pltpu.VMEM((CHUNKS, 64, CHUNK), BF),
            pltpu.VMEM((CHUNKS, 80, CHUNK), BF),
            pltpu.VMEM((64, BLOCK), F32),
            pltpu.VMEM((4, BLOCK), F32),
            pltpu.VMEM((4, 4, BLOCK), F32),
            pltpu.VMEM((BLOCK, 128), BF),
            pltpu.VMEM((2, 4, STRIP, 128), BF),
            pltpu.VMEM((128, BLOCK), F32),
            pltpu.VMEM((8, HALF, 128), BF),
            pltpu.VMEM((2, 4, HALF, 128), BF),
            pltpu.VMEM((N_COL, MSG, 128), BF),
            pltpu.VMEM((N_COL, MSG, 128), BF),
            dma(8), dma(8), dma(16), dma(16), dma(8), dma(8), dma(8), dma(8),
            dma(8), dma(8), dma(4), dma(4), dma(8), dma(2, 4), dma(8), dma(2, 4),
            dma(16), dma(16),
        ],
        compiler_params=pltpu.CompilerParams(
            collective_id=0, has_side_effects=True, vmem_limit_bytes=56 * 2**20
        ),
    )(
        og, zz, turn(query_heads), turn(key_heads), turn(value_heads), conv_weight, out_weight, input_weight,
        *sel,
    )
    return jnp.transpose(result.reshape(TR, TC, SAMPLES, C), (2, 0, 1, 3))


def solution(mesh):
    in_specs = (
        P(None, "row", "col", None),
        P(None, "row", "col", None),
        P("col", "row", None),
        P("col", "row", None),
        P("col", "row", None),
        P(),
        P(),
        P(),
    )
    out_specs = P(None, "row", "col", None)
    return jax.shard_map(shards, mesh=mesh, in_specs=in_specs, out_specs=out_specs, check_vma=False)
```

```python
import functools

import jax
import jax.numpy as jnp
import numpy as np
from jax import lax
from jax.experimental import pallas as pl
from jax.experimental.pallas import tpu as pltpu
from jax.sharding import PartitionSpec as P

BF = jnp.bfloat16
F32 = jnp.float32
SAMPLES, HEADS, HD, C = 8, 4, 64, 256
TR, TC = 3, 6
N_ROW, N_COL = 32, 16
WID = TC * N_COL
STRIP = TR * WID
HALF = STRIP // 2
BLOCK = 8 * STRIP
CHUNK = 256
CHUNKS = BLOCK // CHUNK
PAD = 24
TILE = TR * TC
MESH = pl.DeviceIdType.MESH
FACTOR = HD**-0.5
LOG2E = float(np.log2(np.e))
KAPPA = FACTOR * LOG2E
NT = (((1,), (1,)), ((), ()))


PART_A = 128
PART_B = STRIP - PART_A
HALF_A, HALF_B = PART_A // 2, PART_B // 2
LEN_A = 8 * PART_A
LEN_B = 8 * PART_B
MSG = 40


def selections():
    tile = np.zeros((SAMPLES * PAD, TILE * SAMPLES), np.float32)
    strip = np.zeros((STRIP, N_COL * PAD), np.float32)
    back = np.zeros((N_COL * MSG, 2 * STRIP), np.float32)
    got = np.zeros((2 * TILE * SAMPLES, N_COL * MSG), np.float32)
    got_q = np.zeros((2 * TILE * SAMPLES, N_COL * PAD), np.float32)
    for t in range(TILE):
        for s in range(SAMPLES):
            tile[s * PAD + t, t * SAMPLES + s] = 1.0
        for n in range(N_COL):
            place = (t // TC) * WID + n * TC + t % TC
            strip[place, n * PAD + t] = 1.0
            row = t * SAMPLES + n // 2
            got_q[(n % 2) * TILE * SAMPLES + row, n * PAD + t] = 1.0
            for half in range(2):
                back[n * MSG + half * TILE + t, half * STRIP + place] = 1.0
                got[half * TILE * SAMPLES + row, n * MSG + half * TILE + t] = 1.0
    return tile, strip, back, got, strip.T, got_q


def dot(a, b):
    return jnp.dot(a, b, preferred_element_type=F32)


def dot_nt(a, b):
    return lax.dot_general(a, b, NT, preferred_element_type=F32)


def swap(x):
    return pltpu.roll(x, 64, 1)


def kernel(
    og, zz, qh, kh, vh, eye, *refs,
):
    (
        hbm_cw, hbm_ow, hbm_iw, hbm_tile, hbm_strip, hbm_back, hbm_got, hbm_back_q, hbm_got_q,
        out,
        cw, ow, iw, sel_tile, sel_strip, sel_back, sel_got, sel_back_q, sel_got_q, load_sem,
        xp, gz_keep, ga_s, do_r, qpk, opk, kvpk, q_r, o_r, kv_r, qz, oz, k_t, v_t1,
        o_t, e_s, st_s, lse_s, lse_r, rd_s, rd_r, kv_acc, kvo, kv_part, dq_t, qa, qb,
        qa_part, qb_part, g_s, g_r, h_s, h_r,
        halo_send, halo_recv, a_send, a_recv, q_send, q_recv, o_send, o_recv,
        k_send, k_recv, l_send, l_recv, t_send, t_recv, p_send, p_recv, d_send, d_recv,
        e_send, e_recv, b_send, b_recv, h_send, h_recv,
    ) = refs
    r = lax.axis_index("row")
    c = lax.axis_index("col")
    loads = [
        pltpu.make_async_copy(src, dst, load_sem.at[n])
        for n, (src, dst) in enumerate(
            [(hbm_cw, cw), (hbm_tile, sel_tile), (hbm_ow, ow), (hbm_strip, sel_strip),
             (hbm_iw, iw), (hbm_back, sel_back), (hbm_got, sel_got),
             (hbm_back_q, sel_back_q), (hbm_got_q, sel_got_q)]
        )
    ]
    core = lax.rem(r, 2)
    other = 1 - core
    zi = lax.rem(r // 2, 8)
    xh = r // 16
    zl = lax.rem(zi, 2)
    mq = zi // 2

    def q_peer(o):
        return xh * 16 + (2 * lax.rem(mq + o, 4) + zl) * 2

    def k_peer(o):
        return lax.rem(xh + o // 2, 2) * 16 + (2 * mq + lax.rem(zl + lax.rem(o, 2), 2)) * 2

    def wrap(x, n):
        return lax.rem(x + n, n)

    lanes = lax.broadcasted_iota(jnp.int32, (HALF, 128), 1) < 64
    lanes_strip = lax.broadcasted_iota(jnp.int32, (STRIP, 128), 1) < 64
    lanes_chunk = lax.broadcasted_iota(jnp.int32, (CHUNK, 128), 1) < 64

    barrier = pltpu.get_barrier_semaphore()
    shifts = [(i, j) for i in (-1, 0, 1) for j in (-1, 0, 1) if (i, j) != (0, 0)]
    peers = [(wrap(r + i, N_ROW), wrap(c + j, N_COL)) for i, j in shifts]
    peers += [(r, lax.rem(c + o, N_COL)) for o in range(2, N_COL - 1)]
    for peer in (q_peer, k_peer):
        for o in range(1, 4):
            peers += [(peer(o), c), (peer(o) + 1, c)]
    peers += [(r + 1 - 2 * core, c)]
    for peer in peers:
        pl.semaphore_signal(barrier, inc=1, device_id=peer, device_id_type=MESH)

    for load in loads:
        load.start()

    def halves(x, dst):
        top = jnp.concatenate([x[:HALF_A], x[PART_A : PART_A + HALF_B]], axis=0)
        bottom = jnp.concatenate([x[HALF_A:PART_A], x[PART_A + HALF_B :]], axis=0)
        dst[0] = jnp.where(lanes, top, swap(bottom)).astype(BF)
        dst[1] = jnp.where(lanes, swap(top), bottom).astype(BF)

    for p in range(2):
        kvpk[p] = jnp.concatenate([kh[p], vh[p]], axis=0).T
    halves(jnp.concatenate([qh[0], qh[1]], axis=0).T.astype(F32), qpk)
    xp[1:4, 1:7] = og[...]
    pl.semaphore_wait(barrier, len(peers))

    def push(src, dst, send, recv, peer):
        copy = pltpu.make_async_remote_copy(
            src_ref=src, dst_ref=dst, send_sem=send, recv_sem=recv,
            device_id=peer, device_id_type=MESH,
        )
        return copy

    def rim(shift, width, take):
        if shift == 0:
            return pl.ds(0, width) if take else pl.ds(1, width)
        if take:
            return pl.ds(width - 1, 1) if shift == 1 else pl.ds(0, 1)
        return pl.ds(0, 1) if shift == 1 else pl.ds(width + 1, 1)

    halos = []
    for index, (i, j) in enumerate(shifts):
        halos.append(
            push(
                og.at[rim(i, TR, True), rim(j, TC, True)],
                xp.at[rim(i, TR, False), rim(j, TC, False)],
                halo_send.at[index], halo_recv.at[index],
                (wrap(r + i, N_ROW), wrap(c + j, N_COL)),
            )
        )
    for copy in halos:
        copy.start()

    def gather(src, dst, peer, slot, turn, order, send, recv):
        here = (r + 1 - 2 * core, c)
        dst[slot(0) * 2 + core] = src[core]
        started = [
            push(src.at[other], dst.at[slot(0) * 2 + core], send.at[0], recv.at[0], here)
        ]
        arrivals = {
            0: [push(src.at[0], dst.at[slot(0) * 2 + other], send.at[0], recv.at[0], here)]
        }
        for o in order:
            there = turn(o)
            arrivals[o] = []
            for p in range(2):
                started.append(
                    push(src.at[p], dst.at[slot(o, True) * 2 + core], send.at[2 * o + p],
                         recv.at[2 * there + core], (peer(o) + p, c))
                )
                arrivals[o].append(
                    push(src.at[p], dst.at[slot(o) * 2 + p], send.at[2 * o + p],
                         recv.at[2 * o + p], (peer(o) + p, c))
                )
        return started, arrivals

    def k_slot(o, remote=False):
        return 3 - o

    def q_slot(o, remote=False):
        return mq if remote else lax.rem(mq + o, 4)

    ring = lambda o: (4 - o) % 4
    kv_out, kv_in = gather(kvpk, kv_r, k_peer, k_slot, lambda o: o, (1, 2, 3), k_send, k_recv)
    q_out, q_in = gather(qpk, q_r, q_peer, q_slot, ring, (1, 3, 2), q_send, q_recv)
    for copy in kv_out + q_out[:1]:
        copy.start()

    for load in loads[:3]:
        load.wait()

    for copy in halos:
        copy.wait_recv()
    zero_row = jnp.zeros((1, TC + 2, SAMPLES, C), BF)
    zero_col = jnp.zeros((TR + 2, 1, SAMPLES, C), BF)

    @pl.when(r == 0)
    def _():
        xp[0:1] = zero_row

    @pl.when(r == N_ROW - 1)
    def _():
        xp[TR + 1 : TR + 2] = zero_row

    @pl.when(c == 0)
    def _():
        xp[:, 0:1] = zero_col

    @pl.when(c == N_COL - 1)
    def _():
        xp[:, TC + 1 : TC + 2] = zero_col

    cells = xp[...].astype(F32)
    conv = jnp.zeros((TILE * SAMPLES, C), F32)
    for a in (-1, 0, 1):
        for b in (-1, 0, 1):
            window = cells[1 - a : 1 - a + TR, 1 - b : 1 - b + TC]
            window = window.reshape(TILE * SAMPLES, C).astype(BF)
            conv = conv + dot_nt(window, cw[a + 1, b + 1])
    z = zz[...].astype(F32).reshape(TILE * SAMPLES, C)
    sig = jax.nn.sigmoid(z)
    grad_z = (conv * sig * (1.0 + z * (1.0 - sig))).astype(BF)
    gz_keep[...] = grad_z.astype(F32)
    placed = dot(sel_tile[...], grad_z)
    ga = dot_nt(placed.astype(BF), ow[...])
    for s in range(SAMPLES):
        for b in range(2):
            piece = ga[s * PAD : (s + 1) * PAD, b * 128 : (b + 1) * 128]
            ga_s[2 * s + b] = piece.reshape(3, 8, 128).astype(BF)

    def flat(ref, rows):
        return ref[...].astype(F32).reshape(rows, 128).astype(BF)

    def exchange(src, dst, send, recv):
        dst[c] = src[c]
        started, arrivals = [], []
        for o in range(1, N_COL):
            to, back = lax.rem(c + o, N_COL), lax.rem(c + N_COL - o, N_COL)
            started.append(push(src.at[to], dst.at[c], send.at[o], recv.at[o], (r, to)))
            arrivals.append(
                push(src.at[back], dst.at[back], send.at[o], recv.at[o], (r, back))
            )
        for copy in started:
            copy.start()
        return started, arrivals

    a_out, a_in = exchange(ga_s, do_r, a_send, a_recv)
    for copy in q_out[1:]:
        copy.start()

    def unpack(src, slot, dst, left):
        x = src[slot].astype(F32)
        if left:
            top, bottom = jnp.where(lanes, x, 0.0), jnp.where(lanes, swap(x), 0.0)
        else:
            top, bottom = jnp.where(lanes, 0.0, swap(x)), jnp.where(lanes, 0.0, x)
        top, bottom = top.astype(BF), bottom.astype(BF)
        at = pl.multiple_of(slot * PART_A, PART_A)
        dst[pl.ds(at, HALF_A)] = top[:HALF_A]
        dst[pl.ds(at + HALF_A, HALF_A)] = bottom[:HALF_A]
        at = pl.multiple_of(LEN_A + slot * PART_B, 32)
        dst[pl.ds(at, HALF_B)] = top[HALF_A:]
        dst[pl.ds(at + HALF_B, HALF_B)] = bottom[HALF_A:]

    for o in range(4):
        for copy in kv_in[o]:
            copy.wait_recv()
    keys = kv_r.reshape(BLOCK, 128)
    v_t1[:, 64:80, :] = jnp.ones((CHUNKS, 16, CHUNK), BF)
    for k in range(CHUNKS):
        turned = dot_nt(eye[...], keys[k * CHUNK : (k + 1) * CHUNK]).astype(BF)
        k_t[k] = turned[:64]
        v_t1[k, 0:64, :] = turned[64:]

    def stats_chunk(at):
        scores = dot_nt(keys[...], qz[pl.ds(at, CHUNK)])
        top = jnp.max(scores, axis=0, keepdims=True) * KAPPA
        e = jnp.exp2(scores * KAPPA - top)
        st_s[0:1, pl.ds(at, CHUNK)] = top
        st_s[1:2, pl.ds(at, CHUNK)] = jnp.sum(e, axis=0, keepdims=True)
        eb = e.astype(BF)
        e_s[:, pl.ds(at, CHUNK)] = eb
        acc = jnp.zeros((80, CHUNK), F32)
        for k in range(CHUNKS):
            acc = acc + dot(v_t1[k], eb[k * CHUNK : (k + 1) * CHUNK])
        st_s[2:3, pl.ds(at, CHUNK)] = acc[64:65]
        o_t[:, pl.ds(at, CHUNK)] = acc[:64]

    def stats_member(o):
        for copy in q_in[o]:
            copy.wait_recv()

        for k in range(2):
            unpack(q_r, q_slot(o) * 2 + k, qz, True)
        return o

    def stats_part(o):
        stats_chunk(pl.multiple_of(q_slot(o) * CHUNK, CHUNK))

    stats_part(stats_member(0))
    for copy in a_in:
        copy.wait_recv()
    for load in loads[3:]:
        load.wait()
    halves(dot(sel_strip[...], flat(do_r, N_COL * PAD)), opk)
    o_out, o_in = gather(opk, o_r, q_peer, q_slot, ring, (1, 3, 2), o_send, o_recv)
    for copy in o_out:
        copy.start()
    for o in (1, 3, 2):
        stats_part(stats_member(o))

    def stats_step(k, carry):
        stats_chunk(pl.multiple_of(LEN_A + k * CHUNK, CHUNK))
        return carry

    lax.fori_loop(0, LEN_B // CHUNK, stats_step, 0)

    def share(src, dst, send, recv):
        dst[0] = src[...]
        started, arrivals = [], []
        for o in (2, 1, 3):
            peer = (q_peer(o) + core, c)
            started.append(push(src, dst.at[ring(o)], send.at[o], recv.at[ring(o)], peer))
            arrivals.append(push(src, dst.at[o], send.at[o], recv.at[o], peer))
        for copy in started:
            copy.start()
        return started, arrivals

    lse_s[...] = st_s[0:1] + jnp.log(st_s[1:2]) * LOG2E
    l_out, l_in = share(lse_s, lse_r, l_send, l_recv)
    for o in range(4):
        for copy in o_in[o]:
            copy.wait_recv()
    for k in range(8):
        unpack(o_r, k, oz, False)
    do_t = dot_nt(eye[64:], oz[...])
    rd_s[...] = jnp.sum(o_t[...] * do_t, axis=0, keepdims=True) / st_s[2:3]
    t_out, t_in = share(rd_s, rd_r, t_send, t_recv)
    for copy in l_in:
        copy.wait_recv()
    logs = [lse_r[n] for n in range(4)]
    top = jnp.maximum(jnp.maximum(logs[0], logs[1]), jnp.maximum(logs[2], logs[3]))
    norm = sum(jnp.exp2(log - top) for log in logs)
    log_norm = top + jnp.log(norm) * LOG2E
    rescale = jnp.exp2(st_s[0:1] - log_norm)
    shares = [jnp.exp2(log - log_norm) for log in logs]
    for copy in t_in:
        copy.wait_recv()
    row_dot = sum(share * rd_r[n] for n, share in enumerate(shares))

    dq_t[...] = jnp.zeros_like(dq_t)
    mine = 6 + core

    def part_copy(k):
        at = pl.multiple_of(k * STRIP, 32)
        o = 3 - k // 2
        return push(
            kvo.at[pl.ds(at, STRIP)], kv_part.at[core, o], p_send.at[k],
            p_recv.at[core, o], (k_peer(o) + lax.rem(k, 2), c),
        )

    def grad_pass(lo, width, last):
        part = slice(lo, lo + width)

        def step(j, carry):
            at = pl.multiple_of(j * CHUNK, CHUNK)
            probs = e_s[pl.ds(at, CHUNK), part].astype(F32) * rescale[:, part]
            grad_probs = dot_nt(keys[pl.ds(at, CHUNK)], oz[part])
            grad_scores = (probs * (grad_probs - row_dot[:, part])).astype(BF)
            both = dot(grad_scores, qz[part]) + dot(probs.astype(BF), oz[part])
            dq_t[0:64, part] += dot(k_t[j], grad_scores)
            if not last:
                kv_acc[pl.ds(at, CHUNK)] = both
                return carry
            both = both + kv_acc[pl.ds(at, CHUNK)]
            kvo[pl.ds(at, CHUNK)] = jnp.where(lanes_chunk, both * FACTOR, both).astype(BF)
            k = j - 1

            @pl.when(jnp.logical_and(k >= 0, k != mine))
            def _():
                part_copy(k).start()

            return carry

        lax.fori_loop(0, CHUNKS, step, 0)

    def send_queries(part, half, src, dst, send, recv):
        turned = dq_t[:, part].T * FACTOR
        for k in range(8):
            first = turned[2 * k * half : (2 * k + 1) * half]
            second = turned[(2 * k + 1) * half : (2 * k + 2) * half]
            src[k] = (first + swap(second)).astype(BF)
        dst[core, 0] = src[mq * 2 + core]
        started = [
            push(src.at[q_slot(o) * 2 + p], dst.at[core, ring(o)], send.at[2 * o + p],
                 recv.at[core, ring(o)], (q_peer(o) + p, c))
            for o in (2, 1, 3) for p in range(2)
        ]
        started.append(
            push(src.at[mq * 2 + other], dst.at[core, 0], send.at[0], recv.at[core, 0],
                 (r + 1 - 2 * core, c))
        )
        for copy in started:
            copy.start()
        return started

    grad_pass(LEN_A, LEN_B, False)
    d_out = send_queries(slice(LEN_A, BLOCK), HALF_B, qb, qb_part, d_send, d_recv)
    grad_pass(0, LEN_A, True)
    kv_part[core, 0] = kvo[pl.ds(pl.multiple_of(mine * STRIP, 32), STRIP)]
    d_out += send_queries(slice(0, LEN_A), HALF_A, qa, qa_part, e_send, e_recv)

    def arrive(src, dst, send, recv, peer):
        push(src, dst.at[other, 0], send.at[0], recv.at[other, 0],
             (r + 1 - 2 * core, c)).wait_recv()
        for o in range(1, 4):
            for p in range(2):
                push(src, dst.at[p, o], send.at[0], recv.at[p, o], (peer(o) + p, c)).wait_recv()

    arrive(kvo.at[pl.ds(0, STRIP)], kv_part, p_send, p_recv, k_peer)
    kv0, kv1 = [sum(kv_part[p, n].astype(F32) for n in range(4)) for p in range(2)]
    dk = jnp.where(lanes_strip, kv0, swap(kv1)).astype(BF)
    dv = jnp.where(lanes_strip, swap(kv0), kv1).astype(BF)

    def weight(kind):
        return iw[:, pl.ds(pl.multiple_of(kind * C + lax.rem(c, 2) * 128, 128), 128)]

    projected = (dot_nt(dk, weight(1)) + dot_nt(dv, weight(2))).astype(BF)
    projected = jnp.concatenate([projected[:, :128], projected[:, 128:]], axis=0)
    placed = dot(sel_back[...], projected)
    g_s[...] = placed.reshape(N_COL, MSG // 8, 8, 128).astype(BF)
    b_out, b_in = exchange(g_s, g_r, b_send, b_recv)

    arrive(qb.at[0], qb_part, d_send, d_recv, q_peer)
    arrive(qa.at[0], qa_part, e_send, e_recv, q_peer)

    def unpacked(part, keep):
        q0, q1 = [sum(part[p, n].astype(F32) for n in range(4)) for p in range(2)]
        return [jnp.where(keep, q0, swap(q1)), jnp.where(keep, swap(q0), q1)]

    dq = unpacked(qa_part, lanes[:HALF_A]) + unpacked(qb_part, lanes[:HALF_B])
    placed = dot(sel_back_q[...], jnp.concatenate(dq, axis=0).astype(BF))
    h_s[...] = placed.reshape(N_COL, PAD // 8, 8, 128).astype(BF)
    h_out, h_in = exchange(h_s, h_r, h_send, h_recv)
    rows = TILE * SAMPLES
    for copy in b_in:
        copy.wait_recv()
    sums = dot(sel_got[...], flat(g_r, N_COL * MSG))
    total = gz_keep[...] + jnp.concatenate([sums[:rows], sums[rows:]], axis=1)
    for copy in h_in:
        copy.wait_recv()
    got = dot(sel_got_q[...], flat(h_r, N_COL * PAD)).astype(BF)
    for b in range(2):
        total = total + dot_nt(got[b * rows : (b + 1) * rows], iw[:, b * 128 : (b + 1) * 128])
    out[...] = total.astype(BF)

    for copy in halos + kv_out + q_out + a_out + o_out + l_out + t_out + b_out + h_out:
        copy.wait_send()
    for copy in d_out:
        copy.wait_send()
    for k in range(8):

        @pl.when(k != mine)
        def _():
            part_copy(k).wait_send()


def shards(
    pre_silu, out_grad, query_heads, key_heads, value_heads, conv_weight, out_weight, input_weight
):
    sel = [jnp.asarray(x, BF) for x in selections()]
    turn = lambda x: jnp.transpose(x, (0, 2, 1))
    og = jnp.transpose(out_grad, (1, 2, 0, 3))
    zz = jnp.transpose(pre_silu, (1, 2, 0, 3))
    vmem = pl.BlockSpec(memory_space=pltpu.VMEM)
    dma = lambda *n: pltpu.SemaphoreType.DMA(n)
    result = pl.pallas_call(
        kernel,
        out_shape=jax.ShapeDtypeStruct((TILE * SAMPLES, C), BF),
        in_specs=[vmem] * 6 + [pl.BlockSpec(memory_space=pl.ANY)] * 9,
        out_specs=vmem,
        scratch_shapes=[
            *[pltpu.VMEM(x.shape, BF) for x in (conv_weight, out_weight, input_weight, *sel)],
            dma(9),
            pltpu.VMEM((TR + 2, TC + 2, SAMPLES, C), BF),
            pltpu.VMEM((TILE * SAMPLES, C), F32),
            pltpu.VMEM((N_COL, PAD // 8, 8, 128), BF),
            pltpu.VMEM((N_COL, PAD // 8, 8, 128), BF),
            pltpu.VMEM((2, HALF, 128), BF),
            pltpu.VMEM((2, HALF, 128), BF),
            pltpu.VMEM((2, STRIP, 128), BF),
            pltpu.VMEM((8, HALF, 128), BF),
            pltpu.VMEM((8, HALF, 128), BF),
            pltpu.VMEM((8, STRIP, 128), BF),
            pltpu.VMEM((BLOCK, 128), BF),
            pltpu.VMEM((BLOCK, 128), BF),
            pltpu.VMEM((CHUNKS, 64, CHUNK), BF),
            pltpu.VMEM((CHUNKS, 80, CHUNK), BF),
            pltpu.VMEM((64, BLOCK), F32),
            pltpu.VMEM((BLOCK, BLOCK), BF),
            pltpu.VMEM((4, BLOCK), F32),
            pltpu.VMEM((1, BLOCK), F32),
            pltpu.VMEM((4, 1, BLOCK), F32),
            pltpu.VMEM((1, BLOCK), F32),
            pltpu.VMEM((4, 1, BLOCK), F32),
            pltpu.VMEM((BLOCK, 128), F32),
            pltpu.VMEM((BLOCK, 128), BF),
            pltpu.VMEM((2, 4, STRIP, 128), BF),
            pltpu.VMEM((128, BLOCK), F32),
            pltpu.VMEM((8, HALF_A, 128), BF),
            pltpu.VMEM((8, HALF_B, 128), BF),
            pltpu.VMEM((2, 4, HALF_A, 128), BF),
            pltpu.VMEM((2, 4, HALF_B, 128), BF),
            pltpu.VMEM((N_COL, MSG // 8, 8, 128), BF),
            pltpu.VMEM((N_COL, MSG // 8, 8, 128), BF),
            pltpu.VMEM((N_COL, PAD // 8, 8, 128), BF),
            pltpu.VMEM((N_COL, PAD // 8, 8, 128), BF),
            dma(8), dma(8), dma(16), dma(16), dma(8), dma(8), dma(8), dma(8),
            dma(8), dma(8), dma(4), dma(4), dma(4), dma(4), dma(8), dma(2, 4), dma(8), dma(2, 4),
            dma(8), dma(2, 4), dma(16), dma(16), dma(16), dma(16),
        ],
        compiler_params=pltpu.CompilerParams(
            collective_id=0, has_side_effects=True, vmem_limit_bytes=56 * 2**20
        ),
    )(
        og, zz, turn(query_heads), turn(key_heads), turn(value_heads), jnp.asarray(np.eye(128), BF),
        conv_weight, out_weight, input_weight, *sel,
    )
    return jnp.transpose(result.reshape(TR, TC, SAMPLES, C), (2, 0, 1, 3))


def solution(mesh):
    in_specs = (
        P(None, "row", "col", None),
        P(None, "row", "col", None),
        P("col", "row", None),
        P("col", "row", None),
        P("col", "row", None),
        P(),
        P(),
        P(),
    )
    out_specs = P(None, "row", "col", None)
    return jax.shard_map(shards, mesh=mesh, in_specs=in_specs, out_specs=out_specs, check_vma=False)
```

```python
import functools

import jax
import jax.numpy as jnp
import numpy as np
from jax import lax
from jax.experimental import pallas as pl
from jax.experimental.pallas import tpu as pltpu
from jax.sharding import PartitionSpec as P

BF = jnp.bfloat16
F32 = jnp.float32
SAMPLES, HEADS, HD, C = 8, 4, 64, 256
TR, TC = 3, 6
N_ROW, N_COL = 32, 16
WID = TC * N_COL
STRIP = TR * WID
HALF = STRIP // 2
BLOCK = 8 * STRIP
CHUNK = 256
CHUNKS = BLOCK // CHUNK
PAD = 24
TILE = TR * TC
MESH = pl.DeviceIdType.MESH
FACTOR = HD**-0.5
LOG2E = float(np.log2(np.e))
KAPPA = FACTOR * LOG2E
NT = (((1,), (1,)), ((), ()))


PART_A = 192
PART_B = STRIP - PART_A
HALF_A, HALF_B = PART_A // 2, PART_B // 2
LEN_A = 8 * PART_A
LEN_B = 8 * PART_B
MSG = 40


def selections():
    tile = np.zeros((SAMPLES * PAD, TILE * SAMPLES), np.float32)
    strip = np.zeros((STRIP, N_COL * PAD), np.float32)
    back = np.zeros((N_COL * MSG, 2 * STRIP), np.float32)
    got = np.zeros((2 * TILE * SAMPLES, N_COL * MSG), np.float32)
    for t in range(TILE):
        for s in range(SAMPLES):
            tile[s * PAD + t, t * SAMPLES + s] = 1.0
        for n in range(N_COL):
            place = (t // TC) * WID + n * TC + t % TC
            strip[place, n * PAD + t] = 1.0
            row = t * SAMPLES + n // 2
            for half in range(2):
                back[n * MSG + half * TILE + t, half * STRIP + place] = 1.0
                got[half * TILE * SAMPLES + row, n * MSG + half * TILE + t] = 1.0
    return tile, strip, back, got


def dot(a, b):
    return jnp.dot(a, b, preferred_element_type=F32)


def dot_nt(a, b):
    return lax.dot_general(a, b, NT, preferred_element_type=F32)


def dot_tn(a, b):
    return lax.dot_general(a, b, (((0,), (0,)), ((), ())), preferred_element_type=F32)


def swap(x):
    return pltpu.roll(x, 64, 1)


def kernel(
    og, zz, qh, kh, vh, eye, *refs,
):
    (
        hbm_cw, hbm_ow, hbm_iw, hbm_tile, hbm_strip, hbm_back, hbm_got,
        out,
        cw, ow, iw, sel_tile, sel_strip, sel_back, sel_got, load_sem,
        xp, gz_keep, ga_s, do_r, qpk, opk, kvpk, q_r, o_r, kv_r, qz, oz, k_t, v_t1,
        o_t, e_s, st_s, lse_s, lse_r, rd_s, rd_r, kv_acc, kvo, kv_part, dq_t, qa, qb,
        qa_part, qb_part, g_s, g_r, h_s, h_r,
        halo_send, halo_recv, a_send, a_recv, q_send, q_recv, o_send, o_recv,
        k_send, k_recv, l_send, l_recv, t_send, t_recv, p_send, p_recv, d_send, d_recv,
        e_send, e_recv, b_send, b_recv, h_send, h_recv,
    ) = refs
    r = lax.axis_index("row")
    c = lax.axis_index("col")
    loads = [
        pltpu.make_async_copy(src, dst, load_sem.at[n])
        for n, (src, dst) in enumerate(
            [(hbm_cw, cw), (hbm_tile, sel_tile), (hbm_ow, ow), (hbm_strip, sel_strip),
             (hbm_iw, iw), (hbm_back, sel_back), (hbm_got, sel_got)]
        )
    ]
    core = lax.rem(r, 2)
    other = 1 - core
    zi = lax.rem(r // 2, 8)
    xh = r // 16
    zl = lax.rem(zi, 2)
    mq = zi // 2

    def q_peer(o):
        return xh * 16 + (2 * lax.rem(mq + o, 4) + zl) * 2

    def k_peer(o):
        return lax.rem(xh + o // 2, 2) * 16 + (2 * mq + lax.rem(zl + lax.rem(o, 2), 2)) * 2

    def wrap(x, n):
        return lax.rem(x + n, n)

    lanes = lax.broadcasted_iota(jnp.int32, (HALF, 128), 1) < 64
    lanes_strip = lax.broadcasted_iota(jnp.int32, (STRIP, 128), 1) < 64
    lanes_chunk = lax.broadcasted_iota(jnp.int32, (CHUNK, 128), 1) < 64

    barrier = pltpu.get_barrier_semaphore()
    shifts = [(i, j) for i in (-1, 0, 1) for j in (-1, 0, 1) if (i, j) != (0, 0)]
    peers = [(wrap(r + i, N_ROW), wrap(c + j, N_COL)) for i, j in shifts]
    peers += [(r, lax.rem(c + o, N_COL)) for o in range(2, N_COL - 1)]
    for peer in (q_peer, k_peer):
        for o in range(1, 4):
            peers += [(peer(o), c), (peer(o) + 1, c)]
    peers += [(r + 1 - 2 * core, c)]
    for peer in peers:
        pl.semaphore_signal(barrier, inc=1, device_id=peer, device_id_type=MESH)

    for load in loads:
        load.start()

    def halves(x, dst):
        top = jnp.concatenate([x[:HALF_A], x[PART_A : PART_A + HALF_B]], axis=0)
        bottom = jnp.concatenate([x[HALF_A:PART_A], x[PART_A + HALF_B :]], axis=0)
        dst[0] = jnp.where(lanes, top, swap(bottom)).astype(BF)
        dst[1] = jnp.where(lanes, swap(top), bottom).astype(BF)

    for p in range(2):
        kvpk[p] = jnp.concatenate([kh[p], vh[p]], axis=0).T
    halves(jnp.concatenate([qh[0], qh[1]], axis=0).T.astype(F32), qpk)
    xp[1:4, 1:7] = og[...]
    pl.semaphore_wait(barrier, len(peers))

    def push(src, dst, send, recv, peer):
        copy = pltpu.make_async_remote_copy(
            src_ref=src, dst_ref=dst, send_sem=send, recv_sem=recv,
            device_id=peer, device_id_type=MESH,
        )
        return copy

    def rim(shift, width, take):
        if shift == 0:
            return pl.ds(0, width) if take else pl.ds(1, width)
        if take:
            return pl.ds(width - 1, 1) if shift == 1 else pl.ds(0, 1)
        return pl.ds(0, 1) if shift == 1 else pl.ds(width + 1, 1)

    halos = []
    for index, (i, j) in enumerate(shifts):
        halos.append(
            push(
                og.at[rim(i, TR, True), rim(j, TC, True)],
                xp.at[rim(i, TR, False), rim(j, TC, False)],
                halo_send.at[index], halo_recv.at[index],
                (wrap(r + i, N_ROW), wrap(c + j, N_COL)),
            )
        )
    for copy in halos:
        copy.start()

    def gather(src, dst, peer, slot, turn, order, send, recv):
        here = (r + 1 - 2 * core, c)
        dst[slot(0) * 2 + core] = src[core]
        started = [
            push(src.at[other], dst.at[slot(0) * 2 + core], send.at[0], recv.at[0], here)
        ]
        arrivals = {
            0: [push(src.at[0], dst.at[slot(0) * 2 + other], send.at[0], recv.at[0], here)]
        }
        for o in order:
            there = turn(o)
            arrivals[o] = []
            for p in range(2):
                started.append(
                    push(src.at[p], dst.at[slot(o, True) * 2 + core], send.at[2 * o + p],
                         recv.at[2 * there + core], (peer(o) + p, c))
                )
                arrivals[o].append(
                    push(src.at[p], dst.at[slot(o) * 2 + p], send.at[2 * o + p],
                         recv.at[2 * o + p], (peer(o) + p, c))
                )
        return started, arrivals

    def k_slot(o, remote=False):
        return 3 - o

    def q_slot(o, remote=False):
        return mq if remote else lax.rem(mq + o, 4)

    ring = lambda o: (4 - o) % 4
    kv_out, kv_in = gather(kvpk, kv_r, k_peer, k_slot, lambda o: o, (1, 2, 3), k_send, k_recv)
    q_out, q_in = gather(qpk, q_r, q_peer, q_slot, ring, (1, 3, 2), q_send, q_recv)
    for copy in kv_out + q_out[:1]:
        copy.start()

    for load in loads[:3]:
        load.wait()

    for copy in halos:
        copy.wait_recv()
    zero_row = jnp.zeros((1, TC + 2, SAMPLES, C), BF)
    zero_col = jnp.zeros((TR + 2, 1, SAMPLES, C), BF)

    @pl.when(r == 0)
    def _():
        xp[0:1] = zero_row

    @pl.when(r == N_ROW - 1)
    def _():
        xp[TR + 1 : TR + 2] = zero_row

    @pl.when(c == 0)
    def _():
        xp[:, 0:1] = zero_col

    @pl.when(c == N_COL - 1)
    def _():
        xp[:, TC + 1 : TC + 2] = zero_col

    cells = xp[...].astype(F32)
    conv = jnp.zeros((TILE * SAMPLES, C), F32)
    for a in (-1, 0, 1):
        for b in (-1, 0, 1):
            window = cells[1 - a : 1 - a + TR, 1 - b : 1 - b + TC]
            window = window.reshape(TILE * SAMPLES, C).astype(BF)
            conv = conv + dot_nt(window, cw[a + 1, b + 1])
    z = zz[...].astype(F32).reshape(TILE * SAMPLES, C)
    sig = jax.nn.sigmoid(z)
    grad_z = (conv * sig * (1.0 + z * (1.0 - sig))).astype(BF)
    gz_keep[...] = grad_z.astype(F32)
    placed = dot(sel_tile[...], grad_z)
    ga = dot_nt(placed.astype(BF), ow[...])
    for s in range(SAMPLES):
        for b in range(2):
            piece = ga[s * PAD : (s + 1) * PAD, b * 128 : (b + 1) * 128]
            ga_s[2 * s + b] = piece.reshape(3, 8, 128).astype(BF)

    def flat(ref, rows):
        return ref[...].astype(F32).reshape(rows, 128).astype(BF)

    def exchange(src, dst, send, recv):
        dst[c] = src[c]
        started, arrivals = [], []
        for o in range(1, N_COL):
            to, back = lax.rem(c + o, N_COL), lax.rem(c + N_COL - o, N_COL)
            started.append(push(src.at[to], dst.at[c], send.at[o], recv.at[o], (r, to)))
            arrivals.append(
                push(src.at[back], dst.at[back], send.at[o], recv.at[o], (r, back))
            )
        for copy in started:
            copy.start()
        return started, arrivals

    a_out, a_in = exchange(ga_s, do_r, a_send, a_recv)
    for copy in q_out[1:]:
        copy.start()

    def unpack(src, slot, dst, left):
        x = src[slot].astype(F32)
        if left:
            top, bottom = jnp.where(lanes, x, 0.0), jnp.where(lanes, swap(x), 0.0)
        else:
            top, bottom = jnp.where(lanes, 0.0, swap(x)), jnp.where(lanes, 0.0, x)
        top, bottom = top.astype(BF), bottom.astype(BF)
        at = pl.multiple_of(slot * PART_A, PART_A)
        dst[pl.ds(at, HALF_A)] = top[:HALF_A]
        dst[pl.ds(at + HALF_A, HALF_A)] = bottom[:HALF_A]
        at = pl.multiple_of(LEN_A + slot * PART_B, 32)
        dst[pl.ds(at, HALF_B)] = top[HALF_A:]
        dst[pl.ds(at + HALF_B, HALF_B)] = bottom[HALF_A:]

    for o in range(4):
        for copy in kv_in[o]:
            copy.wait_recv()
    keys = kv_r.reshape(BLOCK, 128)
    v_t1[:, 64:80, :] = jnp.ones((CHUNKS, 16, CHUNK), BF)
    for k in range(CHUNKS):
        turned = dot_nt(eye[...], keys[k * CHUNK : (k + 1) * CHUNK]).astype(BF)
        k_t[k] = turned[:64]
        v_t1[k, 0:64, :] = turned[64:]

    def stats_chunk(at, width):
        here = pl.ds(at, width)
        scores = dot_nt(keys[...], qz[here])
        top = jnp.max(scores, axis=0, keepdims=True) * KAPPA
        e = jnp.exp2(scores * KAPPA - top)
        st_s[0:1, here] = top
        st_s[1:2, here] = jnp.sum(e, axis=0, keepdims=True)
        eb = e.astype(BF)
        e_s[:, here] = eb
        acc = jnp.zeros((80, width), F32)
        for k in range(CHUNKS):
            acc = acc + dot(v_t1[k], eb[k * CHUNK : (k + 1) * CHUNK])
        st_s[2:3, here] = acc[64:65]
        o_t[:, here] = acc[:64]

    def stats_member(o):
        for copy in q_in[o]:
            copy.wait_recv()

        for k in range(2):
            unpack(q_r, q_slot(o) * 2 + k, qz, True)
        return o

    def stats_part(o):
        stats_chunk(pl.multiple_of(q_slot(o) * 2 * PART_A, 128), 2 * PART_A)

    stats_part(stats_member(0))
    for copy in a_in:
        copy.wait_recv()
    for load in loads[3:]:
        load.wait()
    halves(dot(sel_strip[...], flat(do_r, N_COL * PAD)), opk)
    o_out, o_in = gather(opk, o_r, q_peer, q_slot, ring, (1, 3, 2), o_send, o_recv)
    for copy in o_out:
        copy.start()
    for o in (1, 3, 2):
        stats_part(stats_member(o))

    stats_chunk(LEN_A, LEN_B)

    def share(src, dst, send, recv):
        dst[0] = src[...]
        started, arrivals = [], []
        for o in (2, 1, 3):
            peer = (q_peer(o) + core, c)
            started.append(push(src, dst.at[ring(o)], send.at[o], recv.at[ring(o)], peer))
            arrivals.append(push(src, dst.at[o], send.at[o], recv.at[o], peer))
        for copy in started:
            copy.start()
        return started, arrivals

    lse_s[...] = st_s[0:1] + jnp.log(st_s[1:2]) * LOG2E
    l_out, l_in = share(lse_s, lse_r, l_send, l_recv)
    for o in range(4):
        for copy in o_in[o]:
            copy.wait_recv()
    for k in range(8):
        unpack(o_r, k, oz, False)
    do_t = dot_nt(eye[64:], oz[...])
    rd_s[...] = jnp.sum(o_t[...] * do_t, axis=0, keepdims=True) / st_s[2:3]
    t_out, t_in = share(rd_s, rd_r, t_send, t_recv)
    for copy in l_in:
        copy.wait_recv()
    logs = [lse_r[n] for n in range(4)]
    top = jnp.maximum(jnp.maximum(logs[0], logs[1]), jnp.maximum(logs[2], logs[3]))
    norm = sum(jnp.exp2(log - top) for log in logs)
    log_norm = top + jnp.log(norm) * LOG2E
    rescale = jnp.exp2(st_s[0:1] - log_norm)
    shares = [jnp.exp2(log - log_norm) for log in logs]
    for copy in t_in:
        copy.wait_recv()
    row_dot = sum(share * rd_r[n] for n, share in enumerate(shares))

    dq_t[...] = jnp.zeros_like(dq_t)
    mine = 6 + core

    def part_copy(k):
        at = pl.multiple_of(k * STRIP, 32)
        o = 3 - k // 2
        return push(
            kvo.at[pl.ds(at, STRIP)], kv_part.at[core, o], p_send.at[k],
            p_recv.at[core, o], (k_peer(o) + lax.rem(k, 2), c),
        )

    def grad_pass(lo, width, last):
        part = slice(lo, lo + width)

        def step(j, carry):
            at = pl.multiple_of(j * CHUNK, CHUNK)
            probs = e_s[pl.ds(at, CHUNK), part].astype(F32) * rescale[:, part]
            grad_probs = dot_nt(keys[pl.ds(at, CHUNK)], oz[part])
            grad_scores = (probs * (grad_probs - row_dot[:, part])).astype(BF)
            both = dot(grad_scores, qz[part]) + dot(probs.astype(BF), oz[part])
            dq_t[0:64, part] += dot(k_t[j], grad_scores)
            if not last:
                kv_acc[pl.ds(at, CHUNK)] = both
                return carry
            both = both + kv_acc[pl.ds(at, CHUNK)]
            kvo[pl.ds(at, CHUNK)] = jnp.where(lanes_chunk, both * FACTOR, both).astype(BF)
            k = j - 1

            @pl.when(jnp.logical_and(k >= 0, k != mine))
            def _():
                part_copy(k).start()

            return carry

        lax.fori_loop(0, CHUNKS, step, 0, unroll=3)

    def send_queries(part, half, src, dst, send, recv):
        turned = dq_t[:, part].T * FACTOR
        for k in range(8):
            first = turned[2 * k * half : (2 * k + 1) * half]
            second = turned[(2 * k + 1) * half : (2 * k + 2) * half]
            src[k] = (first + swap(second)).astype(BF)
        dst[core, 0] = src[mq * 2 + core]
        started = [
            push(src.at[q_slot(o) * 2 + p], dst.at[core, ring(o)], send.at[2 * o + p],
                 recv.at[core, ring(o)], (q_peer(o) + p, c))
            for o in (2, 1, 3) for p in range(2)
        ]
        started.append(
            push(src.at[mq * 2 + other], dst.at[core, 0], send.at[0], recv.at[core, 0],
                 (r + 1 - 2 * core, c))
        )
        for copy in started:
            copy.start()
        return started

    grad_pass(0, LEN_A, False)
    d_out = send_queries(slice(0, LEN_A), HALF_A, qa, qa_part, d_send, d_recv)
    grad_pass(LEN_A, LEN_B, True)
    kv_part[core, 0] = kvo[pl.ds(pl.multiple_of(mine * STRIP, 32), STRIP)]
    d_out += send_queries(slice(LEN_A, BLOCK), HALF_B, qb, qb_part, e_send, e_recv)

    def arrive(src, dst, send, recv, peer):
        push(src, dst.at[other, 0], send.at[0], recv.at[other, 0],
             (r + 1 - 2 * core, c)).wait_recv()
        for o in range(1, 4):
            for p in range(2):
                push(src, dst.at[p, o], send.at[0], recv.at[p, o], (peer(o) + p, c)).wait_recv()

    arrive(kvo.at[pl.ds(0, STRIP)], kv_part, p_send, p_recv, k_peer)
    kv0, kv1 = [sum(kv_part[p, n].astype(F32) for n in range(4)) for p in range(2)]
    dk = jnp.where(lanes_strip, kv0, swap(kv1)).astype(BF)
    dv = jnp.where(lanes_strip, swap(kv0), kv1).astype(BF)

    def weight(kind):
        return iw[:, pl.ds(pl.multiple_of(kind * C + lax.rem(c, 2) * 128, 128), 128)]

    projected = (dot_nt(dk, weight(1)) + dot_nt(dv, weight(2))).astype(BF)
    projected = jnp.concatenate([projected[:, :128], projected[:, 128:]], axis=0)
    placed = dot(sel_back[...], projected)
    g_s[...] = placed.reshape(N_COL, MSG // 8, 8, 128).astype(BF)
    b_out, b_in = exchange(g_s, g_r, b_send, b_recv)

    arrive(qa.at[0], qa_part, d_send, d_recv, q_peer)
    arrive(qb.at[0], qb_part, e_send, e_recv, q_peer)

    def unpacked(part, keep):
        q0, q1 = [sum(part[p, n].astype(F32) for n in range(4)) for p in range(2)]
        return [jnp.where(keep, q0, swap(q1)), jnp.where(keep, swap(q0), q1)]

    dq = unpacked(qa_part, lanes[:HALF_A]) + unpacked(qb_part, lanes[:HALF_B])
    placed = dot_tn(sel_strip[...], jnp.concatenate(dq, axis=0).astype(BF))
    h_s[...] = placed.reshape(N_COL, PAD // 8, 8, 128).astype(BF)
    h_out, h_in = exchange(h_s, h_r, h_send, h_recv)
    rows = TILE * SAMPLES
    for copy in b_in:
        copy.wait_recv()
    sums = dot(sel_got[...], flat(g_r, N_COL * MSG))
    total = gz_keep[...] + jnp.concatenate([sums[:rows], sums[rows:]], axis=1)
    for copy in h_in:
        copy.wait_recv()
    for b in range(2):
        got = jnp.concatenate([h_r[2 * s + b].astype(F32) for s in range(SAMPLES)], axis=0)
        got = dot_tn(sel_tile[...], got.reshape(SAMPLES * PAD, 128).astype(BF)).astype(BF)
        total = total + dot_nt(got, iw[:, b * 128 : (b + 1) * 128])
    out[...] = total.astype(BF)

    for copy in halos + kv_out + q_out + a_out + o_out + l_out + t_out + b_out + h_out:
        copy.wait_send()
    for copy in d_out:
        copy.wait_send()
    for k in range(8):

        @pl.when(k != mine)
        def _():
            part_copy(k).wait_send()


def shards(
    pre_silu, out_grad, query_heads, key_heads, value_heads, conv_weight, out_weight, input_weight
):
    sel = [jnp.asarray(x, BF) for x in selections()]
    turn = lambda x: jnp.transpose(x, (0, 2, 1))
    og = jnp.transpose(out_grad, (1, 2, 0, 3))
    zz = jnp.transpose(pre_silu, (1, 2, 0, 3))
    vmem = pl.BlockSpec(memory_space=pltpu.VMEM)
    dma = lambda *n: pltpu.SemaphoreType.DMA(n)
    result = pl.pallas_call(
        kernel,
        out_shape=jax.ShapeDtypeStruct((TILE * SAMPLES, C), BF),
        in_specs=[vmem] * 6 + [pl.BlockSpec(memory_space=pl.ANY)] * 7,
        out_specs=vmem,
        scratch_shapes=[
            *[pltpu.VMEM(x.shape, BF) for x in (conv_weight, out_weight, input_weight, *sel)],
            dma(7),
            pltpu.VMEM((TR + 2, TC + 2, SAMPLES, C), BF),
            pltpu.VMEM((TILE * SAMPLES, C), F32),
            pltpu.VMEM((N_COL, PAD // 8, 8, 128), BF),
            pltpu.VMEM((N_COL, PAD // 8, 8, 128), BF),
            pltpu.VMEM((2, HALF, 128), BF),
            pltpu.VMEM((2, HALF, 128), BF),
            pltpu.VMEM((2, STRIP, 128), BF),
            pltpu.VMEM((8, HALF, 128), BF),
            pltpu.VMEM((8, HALF, 128), BF),
            pltpu.VMEM((8, STRIP, 128), BF),
            pltpu.VMEM((BLOCK, 128), BF),
            pltpu.VMEM((BLOCK, 128), BF),
            pltpu.VMEM((CHUNKS, 64, CHUNK), BF),
            pltpu.VMEM((CHUNKS, 80, CHUNK), BF),
            pltpu.VMEM((64, BLOCK), F32),
            pltpu.VMEM((BLOCK, BLOCK), BF),
            pltpu.VMEM((4, BLOCK), F32),
            pltpu.VMEM((1, BLOCK), F32),
            pltpu.VMEM((4, 1, BLOCK), F32),
            pltpu.VMEM((1, BLOCK), F32),
            pltpu.VMEM((4, 1, BLOCK), F32),
            pltpu.VMEM((BLOCK, 128), F32),
            pltpu.VMEM((BLOCK, 128), BF),
            pltpu.VMEM((2, 4, STRIP, 128), BF),
            pltpu.VMEM((128, BLOCK), F32),
            pltpu.VMEM((8, HALF_A, 128), BF),
            pltpu.VMEM((8, HALF_B, 128), BF),
            pltpu.VMEM((2, 4, HALF_A, 128), BF),
            pltpu.VMEM((2, 4, HALF_B, 128), BF),
            pltpu.VMEM((N_COL, MSG // 8, 8, 128), BF),
            pltpu.VMEM((N_COL, MSG // 8, 8, 128), BF),
            pltpu.VMEM((N_COL, PAD // 8, 8, 128), BF),
            pltpu.VMEM((N_COL, PAD // 8, 8, 128), BF),
            dma(8), dma(8), dma(16), dma(16), dma(8), dma(8), dma(8), dma(8),
            dma(8), dma(8), dma(4), dma(4), dma(4), dma(4), dma(8), dma(2, 4), dma(8), dma(2, 4),
            dma(8), dma(2, 4), dma(16), dma(16), dma(16), dma(16),
        ],
        compiler_params=pltpu.CompilerParams(
            collective_id=0, has_side_effects=True, vmem_limit_bytes=56 * 2**20
        ),
    )(
        og, zz, turn(query_heads), turn(key_heads), turn(value_heads), jnp.asarray(np.eye(128), BF),
        conv_weight, out_weight, input_weight, *sel,
    )
    return jnp.transpose(result.reshape(TR, TC, SAMPLES, C), (2, 0, 1, 3))


def solution(mesh):
    in_specs = (
        P(None, "row", "col", None),
        P(None, "row", "col", None),
        P("col", "row", None),
        P("col", "row", None),
        P("col", "row", None),
        P(),
        P(),
        P(),
    )
    out_specs = P(None, "row", "col", None)
    return jax.shard_map(shards, mesh=mesh, in_specs=in_specs, out_specs=out_specs, check_vma=False)
```

```python
import functools

import jax
import jax.numpy as jnp
import numpy as np
from jax import lax
from jax.experimental import pallas as pl
from jax.experimental.pallas import tpu as pltpu
from jax.sharding import PartitionSpec as P

BF = jnp.bfloat16
F32 = jnp.float32
SAMPLES, HEADS, HD, C = 8, 4, 64, 256
TR, TC = 3, 6
N_ROW, N_COL = 32, 16
WID = TC * N_COL
STRIP = TR * WID
HALF = STRIP // 2
BLOCK = 8 * STRIP
CHUNK = 256
CHUNKS = BLOCK // CHUNK
PAD = 24
TILE = TR * TC
MESH = pl.DeviceIdType.MESH
FACTOR = HD**-0.5
LOG2E = float(np.log2(np.e))
KAPPA = FACTOR * LOG2E
NT = (((1,), (1,)), ((), ()))


PART_A = 192
PART_B = STRIP - PART_A
HALF_A, HALF_B = PART_A // 2, PART_B // 2
LEN_A = 8 * PART_A
LEN_B = 8 * PART_B
MSG = 40


def selections():
    tile = np.zeros((SAMPLES * PAD, TILE * SAMPLES), np.float32)
    strip = np.zeros((STRIP, N_COL * PAD), np.float32)
    back = np.zeros((N_COL * MSG, 2 * STRIP), np.float32)
    got = np.zeros((2 * TILE * SAMPLES, N_COL * MSG), np.float32)
    for t in range(TILE):
        for s in range(SAMPLES):
            tile[s * PAD + t, t * SAMPLES + s] = 1.0
        for n in range(N_COL):
            place = (t // TC) * WID + n * TC + t % TC
            strip[place, n * PAD + t] = 1.0
            row = t * SAMPLES + n // 2
            for half in range(2):
                back[n * MSG + half * TILE + t, half * STRIP + place] = 1.0
                got[half * TILE * SAMPLES + row, n * MSG + half * TILE + t] = 1.0
    return tile, strip, back, got


def dot(a, b):
    return jnp.dot(a, b, preferred_element_type=F32)


def dot_nt(a, b):
    return lax.dot_general(a, b, NT, preferred_element_type=F32)


def dot_tn(a, b):
    return lax.dot_general(a, b, (((0,), (0,)), ((), ())), preferred_element_type=F32)


def swap(x):
    return pltpu.roll(x, 64, 1)


def kernel(
    og, zz, qh, kh, vh, eye, *refs,
):
    (
        hbm_cw, hbm_ow, hbm_iw, hbm_tile, hbm_strip, hbm_back, hbm_got,
        out,
        cw, ow, iw, sel_tile, sel_strip, sel_back, sel_got, load_sem,
        xp, gz_keep, ga_s, do_r, qpk, opk, kvpk, q_r, o_r, kv_r, qz, oz, k_t, v_t1,
        o_t, e_s, st_s, lse_s, lse_r, rd_s, rd_r, kv_acc, kvo, kv_part, dq_t, qa, qb,
        qa_part, qb_part, g_s, g_r, h_s, h_r,
        halo_send, halo_recv, a_send, a_recv, q_send, q_recv, o_send, o_recv,
        k_send, k_recv, l_send, l_recv, t_send, t_recv, p_send, p_recv, d_send, d_recv,
        e_send, e_recv, b_send, b_recv, h_send, h_recv,
    ) = refs
    r = lax.axis_index("row")
    c = lax.axis_index("col")
    loads = [
        pltpu.make_async_copy(src, dst, load_sem.at[n])
        for n, (src, dst) in enumerate(
            [(hbm_cw, cw), (hbm_tile, sel_tile), (hbm_ow, ow), (hbm_strip, sel_strip),
             (hbm_iw, iw), (hbm_back, sel_back), (hbm_got, sel_got)]
        )
    ]
    core = lax.rem(r, 2)
    other = 1 - core
    zi = lax.rem(r // 2, 8)
    xh = r // 16
    zl = lax.rem(zi, 2)
    mq = zi // 2

    def q_peer(o):
        return xh * 16 + (2 * lax.rem(mq + o, 4) + zl) * 2

    def k_peer(o):
        return lax.rem(xh + o // 2, 2) * 16 + (2 * mq + lax.rem(zl + lax.rem(o, 2), 2)) * 2

    def wrap(x, n):
        return lax.rem(x + n, n)

    lanes = lax.broadcasted_iota(jnp.int32, (HALF, 128), 1) < 64
    lanes_strip = lax.broadcasted_iota(jnp.int32, (STRIP, 128), 1) < 64
    lanes_chunk = lax.broadcasted_iota(jnp.int32, (CHUNK, 128), 1) < 64

    barrier = pltpu.get_barrier_semaphore()
    shifts = [(i, j) for i in (-1, 0, 1) for j in (-1, 0, 1) if (i, j) != (0, 0)]
    peers = [(wrap(r + i, N_ROW), wrap(c + j, N_COL)) for i, j in shifts]
    peers += [(r, lax.rem(c + o, N_COL)) for o in range(2, N_COL - 1)]
    for peer in (q_peer, k_peer):
        for o in range(1, 4):
            peers += [(peer(o), c), (peer(o) + 1, c)]
    peers += [(r + 1 - 2 * core, c)]
    for peer in peers:
        pl.semaphore_signal(barrier, inc=1, device_id=peer, device_id_type=MESH)

    for load in loads:
        load.start()

    def halves(x, dst):
        top = jnp.concatenate([x[:HALF_A], x[PART_A : PART_A + HALF_B]], axis=0)
        bottom = jnp.concatenate([x[HALF_A:PART_A], x[PART_A + HALF_B :]], axis=0)
        dst[0] = jnp.where(lanes, top, swap(bottom)).astype(BF)
        dst[1] = jnp.where(lanes, swap(top), bottom).astype(BF)

    for p in range(2):
        kvpk[p] = jnp.concatenate([kh[p], vh[p]], axis=0).T
    halves(jnp.concatenate([qh[0], qh[1]], axis=0).T.astype(F32), qpk)
    xp[1:4, 1:7] = og[...]
    pl.semaphore_wait(barrier, len(peers))

    def push(src, dst, send, recv, peer):
        copy = pltpu.make_async_remote_copy(
            src_ref=src, dst_ref=dst, send_sem=send, recv_sem=recv,
            device_id=peer, device_id_type=MESH,
        )
        return copy

    def rim(shift, width, take):
        if shift == 0:
            return pl.ds(0, width) if take else pl.ds(1, width)
        if take:
            return pl.ds(width - 1, 1) if shift == 1 else pl.ds(0, 1)
        return pl.ds(0, 1) if shift == 1 else pl.ds(width + 1, 1)

    halos = []
    for index, (i, j) in enumerate(shifts):
        halos.append(
            push(
                og.at[rim(i, TR, True), rim(j, TC, True)],
                xp.at[rim(i, TR, False), rim(j, TC, False)],
                halo_send.at[index], halo_recv.at[index],
                (wrap(r + i, N_ROW), wrap(c + j, N_COL)),
            )
        )
    for copy in halos:
        copy.start()

    def gather(src, dst, peer, slot, turn, order, send, recv):
        here = (r + 1 - 2 * core, c)
        dst[slot(0) * 2 + core] = src[core]
        started = [
            push(src.at[other], dst.at[slot(0) * 2 + core], send.at[0], recv.at[0], here)
        ]
        arrivals = {
            0: [push(src.at[0], dst.at[slot(0) * 2 + other], send.at[0], recv.at[0], here)]
        }
        for o in order:
            there = turn(o)
            arrivals[o] = []
            for p in range(2):
                started.append(
                    push(src.at[p], dst.at[slot(o, True) * 2 + core], send.at[2 * o + p],
                         recv.at[2 * there + core], (peer(o) + p, c))
                )
                arrivals[o].append(
                    push(src.at[p], dst.at[slot(o) * 2 + p], send.at[2 * o + p],
                         recv.at[2 * o + p], (peer(o) + p, c))
                )
        return started, arrivals

    def k_slot(o, remote=False):
        return 3 - o

    def q_slot(o, remote=False):
        return mq if remote else lax.rem(mq + o, 4)

    ring = lambda o: (4 - o) % 4
    kv_out, kv_in = gather(kvpk, kv_r, k_peer, k_slot, lambda o: o, (1, 2, 3), k_send, k_recv)
    q_out, q_in = gather(qpk, q_r, q_peer, q_slot, ring, (1, 3, 2), q_send, q_recv)
    for copy in kv_out + q_out[:5]:
        copy.start()

    for load in loads[:3]:
        load.wait()

    for copy in halos:
        copy.wait_recv()
    zero_row = jnp.zeros((1, TC + 2, SAMPLES, C), BF)
    zero_col = jnp.zeros((TR + 2, 1, SAMPLES, C), BF)

    @pl.when(r == 0)
    def _():
        xp[0:1] = zero_row

    @pl.when(r == N_ROW - 1)
    def _():
        xp[TR + 1 : TR + 2] = zero_row

    @pl.when(c == 0)
    def _():
        xp[:, 0:1] = zero_col

    @pl.when(c == N_COL - 1)
    def _():
        xp[:, TC + 1 : TC + 2] = zero_col

    cells = xp[...].astype(F32)
    conv = jnp.zeros((TILE * SAMPLES, C), F32)
    for a in (-1, 0, 1):
        for b in (-1, 0, 1):
            window = cells[1 - a : 1 - a + TR, 1 - b : 1 - b + TC]
            window = window.reshape(TILE * SAMPLES, C).astype(BF)
            conv = conv + dot_nt(window, cw[a + 1, b + 1])
    z = zz[...].astype(F32).reshape(TILE * SAMPLES, C)
    sig = jax.nn.sigmoid(z)
    grad_z = (conv * sig * (1.0 + z * (1.0 - sig))).astype(BF)
    gz_keep[...] = grad_z.astype(F32)
    placed = dot(sel_tile[...], grad_z)
    ga = dot_nt(placed.astype(BF), ow[...])
    for s in range(SAMPLES):
        for b in range(2):
            piece = ga[s * PAD : (s + 1) * PAD, b * 128 : (b + 1) * 128]
            ga_s[2 * s + b] = piece.reshape(3, 8, 128).astype(BF)

    def flat(ref, rows):
        return ref[...].astype(F32).reshape(rows, 128).astype(BF)

    def exchange(src, dst, send, recv):
        dst[c] = src[c]
        started, arrivals = [], []
        for o in range(1, N_COL):
            to, back = lax.rem(c + o, N_COL), lax.rem(c + N_COL - o, N_COL)
            started.append(push(src.at[to], dst.at[c], send.at[o], recv.at[o], (r, to)))
            arrivals.append(
                push(src.at[back], dst.at[back], send.at[o], recv.at[o], (r, back))
            )
        for copy in started:
            copy.start()
        return started, arrivals

    a_out, a_in = exchange(ga_s, do_r, a_send, a_recv)
    for copy in q_out[5:]:
        copy.start()

    def unpack(src, slot, dst, left):
        x = src[slot].astype(F32)
        if left:
            top, bottom = jnp.where(lanes, x, 0.0), jnp.where(lanes, swap(x), 0.0)
        else:
            top, bottom = jnp.where(lanes, 0.0, swap(x)), jnp.where(lanes, 0.0, x)
        top, bottom = top.astype(BF), bottom.astype(BF)
        at = pl.multiple_of(slot * PART_A, PART_A)
        dst[pl.ds(at, HALF_A)] = top[:HALF_A]
        dst[pl.ds(at + HALF_A, HALF_A)] = bottom[:HALF_A]
        at = pl.multiple_of(LEN_A + slot * PART_B, 32)
        dst[pl.ds(at, HALF_B)] = top[HALF_A:]
        dst[pl.ds(at + HALF_B, HALF_B)] = bottom[HALF_A:]

    for o in range(4):
        for copy in kv_in[o]:
            copy.wait_recv()
    keys = kv_r.reshape(BLOCK, 128)
    v_t1[:, 64:80, :] = jnp.ones((CHUNKS, 16, CHUNK), BF)
    for k in range(CHUNKS):
        turned = dot_nt(eye[...], keys[k * CHUNK : (k + 1) * CHUNK]).astype(BF)
        k_t[k] = turned[:64]
        v_t1[k, 0:64, :] = turned[64:]

    for copy in a_in:
        copy.wait_recv()
    for load in loads[3:]:
        load.wait()
    halves(dot(sel_strip[...], flat(do_r, N_COL * PAD)), opk)
    o_out, o_in = gather(opk, o_r, q_peer, q_slot, ring, (1, 3, 2), o_send, o_recv)
    for copy in o_out:
        copy.start()

    def stats_chunk(at, width):
        here = pl.ds(at, width)
        scores = dot_nt(keys[...], qz[here])
        top = jnp.max(scores, axis=0, keepdims=True) * KAPPA
        e = jnp.exp2(scores * KAPPA - top)
        st_s[0:1, here] = top
        st_s[1:2, here] = jnp.sum(e, axis=0, keepdims=True)
        eb = e.astype(BF)
        e_s[:, here] = eb
        acc = jnp.zeros((80, width), F32)
        for k in range(CHUNKS):
            acc = acc + dot(v_t1[k], eb[k * CHUNK : (k + 1) * CHUNK])
        st_s[2:3, here] = acc[64:65]
        o_t[:, here] = acc[:64]

    def stats_member(o):
        for copy in q_in[o]:
            copy.wait_recv()

        for k in range(2):
            unpack(q_r, q_slot(o) * 2 + k, qz, True)
        return o

    def stats_part(o):
        stats_chunk(pl.multiple_of(q_slot(o) * 2 * PART_A, 128), 2 * PART_A)

    for o in (0, 1, 3, 2):
        stats_part(stats_member(o))

    stats_chunk(LEN_A, LEN_B)

    def share(src, dst, send, recv):
        dst[0] = src[...]
        started, arrivals = [], []
        for o in (2, 1, 3):
            peer = (q_peer(o) + core, c)
            started.append(push(src, dst.at[ring(o)], send.at[o], recv.at[ring(o)], peer))
            arrivals.append(push(src, dst.at[o], send.at[o], recv.at[o], peer))
        for copy in started:
            copy.start()
        return started, arrivals

    lse_s[...] = st_s[0:1] + jnp.log(st_s[1:2]) * LOG2E
    l_out, l_in = share(lse_s, lse_r, l_send, l_recv)
    for o in range(4):
        for copy in o_in[o]:
            copy.wait_recv()
    for k in range(8):
        unpack(o_r, k, oz, False)
    do_t = dot_nt(eye[64:], oz[...])
    rd_s[...] = jnp.sum(o_t[...] * do_t, axis=0, keepdims=True) / st_s[2:3]
    t_out, t_in = share(rd_s, rd_r, t_send, t_recv)
    for copy in l_in:
        copy.wait_recv()
    logs = [lse_r[n] for n in range(4)]
    top = jnp.maximum(jnp.maximum(logs[0], logs[1]), jnp.maximum(logs[2], logs[3]))
    norm = sum(jnp.exp2(log - top) for log in logs)
    log_norm = top + jnp.log(norm) * LOG2E
    rescale = jnp.exp2(st_s[0:1] - log_norm)
    shares = [jnp.exp2(log - log_norm) for log in logs]
    for copy in t_in:
        copy.wait_recv()
    row_dot = sum(share * rd_r[n] for n, share in enumerate(shares))

    dq_t[...] = jnp.zeros_like(dq_t)
    mine = 6 + core

    def part_copy(k):
        at = pl.multiple_of(k * STRIP, 32)
        o = 3 - k // 2
        return push(
            kvo.at[pl.ds(at, STRIP)], kv_part.at[core, o], p_send.at[k],
            p_recv.at[core, o], (k_peer(o) + lax.rem(k, 2), c),
        )

    def grad_pass(lo, width, last):
        part = slice(lo, lo + width)

        def step(j, carry):
            at = pl.multiple_of(j * CHUNK, CHUNK)
            probs = e_s[pl.ds(at, CHUNK), part].astype(F32) * rescale[:, part]
            grad_probs = dot_nt(keys[pl.ds(at, CHUNK)], oz[part])
            grad_scores = (probs * (grad_probs - row_dot[:, part])).astype(BF)
            both = dot(grad_scores, qz[part]) + dot(probs.astype(BF), oz[part])
            dq_t[0:64, part] += dot(k_t[j], grad_scores)
            if not last:
                kv_acc[pl.ds(at, CHUNK)] = both
                return carry
            both = both + kv_acc[pl.ds(at, CHUNK)]
            kvo[pl.ds(at, CHUNK)] = jnp.where(lanes_chunk, both * FACTOR, both).astype(BF)
            k = j - 1

            @pl.when(jnp.logical_and(k >= 0, k != mine))
            def _():
                part_copy(k).start()

            return carry

        lax.fori_loop(0, CHUNKS, step, 0, unroll=3)

    def send_queries(part, half, src, dst, send, recv):
        turned = dq_t[:, part].T * FACTOR
        for k in range(8):
            first = turned[2 * k * half : (2 * k + 1) * half]
            second = turned[(2 * k + 1) * half : (2 * k + 2) * half]
            src[k] = (first + swap(second)).astype(BF)
        dst[core, 0] = src[mq * 2 + core]
        started = [
            push(src.at[q_slot(o) * 2 + p], dst.at[core, ring(o)], send.at[2 * o + p],
                 recv.at[core, ring(o)], (q_peer(o) + p, c))
            for o in (2, 1, 3) for p in range(2)
        ]
        started.append(
            push(src.at[mq * 2 + other], dst.at[core, 0], send.at[0], recv.at[core, 0],
                 (r + 1 - 2 * core, c))
        )
        for copy in started:
            copy.start()
        return started

    grad_pass(0, LEN_A, False)
    d_out = send_queries(slice(0, LEN_A), HALF_A, qa, qa_part, d_send, d_recv)
    grad_pass(LEN_A, LEN_B, True)
    kv_part[core, 0] = kvo[pl.ds(pl.multiple_of(mine * STRIP, 32), STRIP)]
    d_out += send_queries(slice(LEN_A, BLOCK), HALF_B, qb, qb_part, e_send, e_recv)

    def arrive(src, dst, send, recv, peer):
        push(src, dst.at[other, 0], send.at[0], recv.at[other, 0],
             (r + 1 - 2 * core, c)).wait_recv()
        for o in range(1, 4):
            for p in range(2):
                push(src, dst.at[p, o], send.at[0], recv.at[p, o], (peer(o) + p, c)).wait_recv()

    arrive(kvo.at[pl.ds(0, STRIP)], kv_part, p_send, p_recv, k_peer)
    kv0, kv1 = [sum(kv_part[p, n].astype(F32) for n in range(4)) for p in range(2)]
    dk = jnp.where(lanes_strip, kv0, swap(kv1)).astype(BF)
    dv = jnp.where(lanes_strip, swap(kv0), kv1).astype(BF)

    def weight(kind):
        return iw[:, pl.ds(pl.multiple_of(kind * C + lax.rem(c, 2) * 128, 128), 128)]

    projected = (dot_nt(dk, weight(1)) + dot_nt(dv, weight(2))).astype(BF)
    projected = jnp.concatenate([projected[:, :128], projected[:, 128:]], axis=0)
    placed = dot(sel_back[...], projected)
    g_s[...] = placed.reshape(N_COL, MSG // 8, 8, 128).astype(BF)
    b_out, b_in = exchange(g_s, g_r, b_send, b_recv)

    arrive(qa.at[0], qa_part, d_send, d_recv, q_peer)
    arrive(qb.at[0], qb_part, e_send, e_recv, q_peer)

    def unpacked(part, keep):
        q0, q1 = [sum(part[p, n].astype(F32) for n in range(4)) for p in range(2)]
        return [jnp.where(keep, q0, swap(q1)), jnp.where(keep, swap(q0), q1)]

    dq = unpacked(qa_part, lanes[:HALF_A]) + unpacked(qb_part, lanes[:HALF_B])
    placed = dot_tn(sel_strip[...], jnp.concatenate(dq, axis=0).astype(BF))
    h_s[...] = placed.reshape(N_COL, PAD // 8, 8, 128).astype(BF)
    h_out, h_in = exchange(h_s, h_r, h_send, h_recv)
    rows = TILE * SAMPLES
    for copy in b_in:
        copy.wait_recv()
    sums = dot(sel_got[...], flat(g_r, N_COL * MSG))
    total = gz_keep[...] + jnp.concatenate([sums[:rows], sums[rows:]], axis=1)
    for copy in h_in:
        copy.wait_recv()
    for b in range(2):
        got = jnp.concatenate([h_r[2 * s + b].astype(F32) for s in range(SAMPLES)], axis=0)
        got = dot_tn(sel_tile[...], got.reshape(SAMPLES * PAD, 128).astype(BF)).astype(BF)
        total = total + dot_nt(got, iw[:, b * 128 : (b + 1) * 128])
    out[...] = total.astype(BF)

    for copy in halos + kv_out + q_out + a_out + o_out + l_out + t_out + b_out + h_out:
        copy.wait_send()
    for copy in d_out:
        copy.wait_send()
    for k in range(8):

        @pl.when(k != mine)
        def _():
            part_copy(k).wait_send()


def shards(
    pre_silu, out_grad, query_heads, key_heads, value_heads, conv_weight, out_weight, input_weight
):
    sel = [jnp.asarray(x, BF) for x in selections()]
    turn = lambda x: jnp.transpose(x, (0, 2, 1))
    og = jnp.transpose(out_grad, (1, 2, 0, 3))
    zz = jnp.transpose(pre_silu, (1, 2, 0, 3))
    vmem = pl.BlockSpec(memory_space=pltpu.VMEM)
    dma = lambda *n: pltpu.SemaphoreType.DMA(n)
    result = pl.pallas_call(
        kernel,
        out_shape=jax.ShapeDtypeStruct((TILE * SAMPLES, C), BF),
        in_specs=[vmem] * 6 + [pl.BlockSpec(memory_space=pl.ANY)] * 7,
        out_specs=vmem,
        scratch_shapes=[
            *[pltpu.VMEM(x.shape, BF) for x in (conv_weight, out_weight, input_weight, *sel)],
            dma(7),
            pltpu.VMEM((TR + 2, TC + 2, SAMPLES, C), BF),
            pltpu.VMEM((TILE * SAMPLES, C), F32),
            pltpu.VMEM((N_COL, PAD // 8, 8, 128), BF),
            pltpu.VMEM((N_COL, PAD // 8, 8, 128), BF),
            pltpu.VMEM((2, HALF, 128), BF),
            pltpu.VMEM((2, HALF, 128), BF),
            pltpu.VMEM((2, STRIP, 128), BF),
            pltpu.VMEM((8, HALF, 128), BF),
            pltpu.VMEM((8, HALF, 128), BF),
            pltpu.VMEM((8, STRIP, 128), BF),
            pltpu.VMEM((BLOCK, 128), BF),
            pltpu.VMEM((BLOCK, 128), BF),
            pltpu.VMEM((CHUNKS, 64, CHUNK), BF),
            pltpu.VMEM((CHUNKS, 80, CHUNK), BF),
            pltpu.VMEM((64, BLOCK), F32),
            pltpu.VMEM((BLOCK, BLOCK), BF),
            pltpu.VMEM((4, BLOCK), F32),
            pltpu.VMEM((1, BLOCK), F32),
            pltpu.VMEM((4, 1, BLOCK), F32),
            pltpu.VMEM((1, BLOCK), F32),
            pltpu.VMEM((4, 1, BLOCK), F32),
            pltpu.VMEM((BLOCK, 128), F32),
            pltpu.VMEM((BLOCK, 128), BF),
            pltpu.VMEM((2, 4, STRIP, 128), BF),
            pltpu.VMEM((128, BLOCK), F32),
            pltpu.VMEM((8, HALF_A, 128), BF),
            pltpu.VMEM((8, HALF_B, 128), BF),
            pltpu.VMEM((2, 4, HALF_A, 128), BF),
            pltpu.VMEM((2, 4, HALF_B, 128), BF),
            pltpu.VMEM((N_COL, MSG // 8, 8, 128), BF),
            pltpu.VMEM((N_COL, MSG // 8, 8, 128), BF),
            pltpu.VMEM((N_COL, PAD // 8, 8, 128), BF),
            pltpu.VMEM((N_COL, PAD // 8, 8, 128), BF),
            dma(8), dma(8), dma(16), dma(16), dma(8), dma(8), dma(8), dma(8),
            dma(8), dma(8), dma(4), dma(4), dma(4), dma(4), dma(8), dma(2, 4), dma(8), dma(2, 4),
            dma(8), dma(2, 4), dma(16), dma(16), dma(16), dma(16),
        ],
        compiler_params=pltpu.CompilerParams(
            collective_id=0, has_side_effects=True, vmem_limit_bytes=56 * 2**20
        ),
    )(
        og, zz, turn(query_heads), turn(key_heads), turn(value_heads), jnp.asarray(np.eye(128), BF),
        conv_weight, out_weight, input_weight, *sel,
    )
    return jnp.transpose(result.reshape(TR, TC, SAMPLES, C), (2, 0, 1, 3))


def solution(mesh):
    in_specs = (
        P(None, "row", "col", None),
        P(None, "row", "col", None),
        P("col", "row", None),
        P("col", "row", None),
        P("col", "row", None),
        P(),
        P(),
        P(),
    )
    out_specs = P(None, "row", "col", None)
    return jax.shard_map(shards, mesh=mesh, in_specs=in_specs, out_specs=out_specs, check_vma=False)
```

```python
import functools

import jax
import jax.numpy as jnp
import numpy as np
from jax import lax
from jax.experimental import pallas as pl
from jax.experimental.pallas import tpu as pltpu
from jax.sharding import PartitionSpec as P

BF = jnp.bfloat16
F32 = jnp.float32
SAMPLES, HEADS, HD, C = 8, 4, 64, 256
TR, TC = 3, 6
N_ROW, N_COL = 32, 16
WID = TC * N_COL
STRIP = TR * WID
HALF = STRIP // 2
BLOCK = 8 * STRIP
CHUNK = 256
CHUNKS = BLOCK // CHUNK
PAD = 24
TILE = TR * TC
MESH = pl.DeviceIdType.MESH
FACTOR = HD**-0.5
LOG2E = float(np.log2(np.e))
KAPPA = FACTOR * LOG2E
NT = (((1,), (1,)), ((), ()))


PART_A = 192
PART_B = STRIP - PART_A
HALF_A, HALF_B = PART_A // 2, PART_B // 2
LEN_A = 8 * PART_A
LEN_B = 8 * PART_B
MSG = 40


def selections():
    tile = np.zeros((SAMPLES * PAD, TILE * SAMPLES), np.float32)
    strip = np.zeros((STRIP, N_COL * PAD), np.float32)
    back = np.zeros((N_COL * MSG, 2 * STRIP), np.float32)
    got = np.zeros((2 * TILE * SAMPLES, N_COL * MSG), np.float32)
    for t in range(TILE):
        for s in range(SAMPLES):
            tile[s * PAD + t, t * SAMPLES + s] = 1.0
        for n in range(N_COL):
            place = (t // TC) * WID + n * TC + t % TC
            strip[place, n * PAD + t] = 1.0
            row = t * SAMPLES + n // 2
            for half in range(2):
                back[n * MSG + half * TILE + t, half * STRIP + place] = 1.0
                got[half * TILE * SAMPLES + row, n * MSG + half * TILE + t] = 1.0
    row_back = np.zeros((N_COL * 8, PART_B), np.float32)
    row_got = np.zeros((TC * SAMPLES, SAMPLES * 8), np.float32)
    for t in range(TC):
        for n in range(N_COL):
            row_back[n * 8 + t, n * TC + t] = 1.0
        for s in range(SAMPLES):
            row_got[t * SAMPLES + s, s * 8 + t] = 1.0
    return tile, strip, back, got, row_back, row_got


def dot(a, b):
    return jnp.dot(a, b, preferred_element_type=F32)


def dot_nt(a, b):
    return lax.dot_general(a, b, NT, preferred_element_type=F32)


def swap(x):
    return pltpu.roll(x, 64, 1)


def kernel(
    og, zz, qh, kh, vh, eye, *refs,
):
    (
        hbm_cw, hbm_ow, hbm_iw, hbm_tile, hbm_strip, hbm_back, hbm_got, hbm_row_back, hbm_row_got,
        out,
        cw, ow, iw, sel_tile, sel_strip, sel_back, sel_got, row_back, row_got, load_sem,
        xp, gz_keep, ga_s, do_r, qpk, opk, kvpk, q_r, o_r, kv_r, qz, oz, k_t, v_t1,
        o_t, e_s, st_s, lse_s, lse_r, rd_s, rd_r, kv_acc, kvo, kv_part, dq_t, qa, qb,
        qa_part, qb_part, g_s, g_r, h_s, h_r,
        halo_send, halo_recv, a_send, a_recv, q_send, q_recv, o_send, o_recv,
        k_send, k_recv, l_send, l_recv, t_send, t_recv, p_send, p_recv, d_send, d_recv,
        e_send, e_recv, b_send, b_recv, h_send, h_recv,
    ) = refs
    r = lax.axis_index("row")
    c = lax.axis_index("col")
    loads = [
        pltpu.make_async_copy(src, dst, load_sem.at[n])
        for n, (src, dst) in enumerate(
            [(hbm_cw, cw), (hbm_tile, sel_tile), (hbm_ow, ow), (hbm_strip, sel_strip),
             (hbm_iw, iw), (hbm_back, sel_back), (hbm_got, sel_got),
             (hbm_row_back, row_back), (hbm_row_got, row_got)]
        )
    ]
    core = lax.rem(r, 2)
    other = 1 - core
    zi = lax.rem(r // 2, 8)
    xh = r // 16
    zl = lax.rem(zi, 2)
    mq = zi // 2

    def q_peer(o):
        return xh * 16 + (2 * lax.rem(mq + o, 4) + zl) * 2

    def k_peer(o):
        return lax.rem(xh + o // 2, 2) * 16 + (2 * mq + lax.rem(zl + lax.rem(o, 2), 2)) * 2

    def wrap(x, n):
        return lax.rem(x + n, n)

    lanes = lax.broadcasted_iota(jnp.int32, (HALF, 128), 1) < 64
    lanes_strip = lax.broadcasted_iota(jnp.int32, (STRIP, 128), 1) < 64
    lanes_chunk = lax.broadcasted_iota(jnp.int32, (CHUNK, 128), 1) < 64

    barrier = pltpu.get_barrier_semaphore()
    shifts = [(i, j) for i in (-1, 0, 1) for j in (-1, 0, 1) if (i, j) != (0, 0)]
    peers = [(wrap(r + i, N_ROW), wrap(c + j, N_COL)) for i, j in shifts]
    peers += [(r, lax.rem(c + o, N_COL)) for o in range(2, N_COL - 1)]
    for peer in (q_peer, k_peer):
        for o in range(1, 4):
            peers += [(peer(o), c), (peer(o) + 1, c)]
    peers += [(r + 1 - 2 * core, c)]
    for peer in peers:
        pl.semaphore_signal(barrier, inc=1, device_id=peer, device_id_type=MESH)

    for load in loads:
        load.start()

    def halves(x, dst):
        top = jnp.concatenate([x[:HALF_A], x[PART_A : PART_A + HALF_B]], axis=0)
        bottom = jnp.concatenate([x[HALF_A:PART_A], x[PART_A + HALF_B :]], axis=0)
        dst[0] = jnp.where(lanes, top, swap(bottom)).astype(BF)
        dst[1] = jnp.where(lanes, swap(top), bottom).astype(BF)

    for p in range(2):
        kvpk[p] = jnp.concatenate([kh[p], vh[p]], axis=0).T
    halves(jnp.concatenate([qh[0], qh[1]], axis=0).T.astype(F32), qpk)
    xp[1:4, 1:7] = og[...]
    pl.semaphore_wait(barrier, len(peers))

    def push(src, dst, send, recv, peer):
        copy = pltpu.make_async_remote_copy(
            src_ref=src, dst_ref=dst, send_sem=send, recv_sem=recv,
            device_id=peer, device_id_type=MESH,
        )
        return copy

    def rim(shift, width, take):
        if shift == 0:
            return pl.ds(0, width) if take else pl.ds(1, width)
        if take:
            return pl.ds(width - 1, 1) if shift == 1 else pl.ds(0, 1)
        return pl.ds(0, 1) if shift == 1 else pl.ds(width + 1, 1)

    halos = []
    for index, (i, j) in enumerate(shifts):
        halos.append(
            push(
                og.at[rim(i, TR, True), rim(j, TC, True)],
                xp.at[rim(i, TR, False), rim(j, TC, False)],
                halo_send.at[index], halo_recv.at[index],
                (wrap(r + i, N_ROW), wrap(c + j, N_COL)),
            )
        )
    for copy in halos:
        copy.start()

    def gather(src, dst, peer, slot, turn, order, send, recv):
        here = (r + 1 - 2 * core, c)
        dst[slot(0) * 2 + core] = src[core]
        started = [
            push(src.at[other], dst.at[slot(0) * 2 + core], send.at[0], recv.at[0], here)
        ]
        arrivals = {
            0: [push(src.at[0], dst.at[slot(0) * 2 + other], send.at[0], recv.at[0], here)]
        }
        for o in order:
            there = turn(o)
            arrivals[o] = []
            for p in range(2):
                started.append(
                    push(src.at[p], dst.at[slot(o, True) * 2 + core], send.at[2 * o + p],
                         recv.at[2 * there + core], (peer(o) + p, c))
                )
                arrivals[o].append(
                    push(src.at[p], dst.at[slot(o) * 2 + p], send.at[2 * o + p],
                         recv.at[2 * o + p], (peer(o) + p, c))
                )
        return started, arrivals

    def k_slot(o, remote=False):
        return 3 - o

    def q_slot(o, remote=False):
        return mq if remote else lax.rem(mq + o, 4)

    ring = lambda o: (4 - o) % 4
    kv_out, kv_in = gather(kvpk, kv_r, k_peer, k_slot, lambda o: o, (1, 2, 3), k_send, k_recv)
    q_out, q_in = gather(qpk, q_r, q_peer, q_slot, ring, (1, 3, 2), q_send, q_recv)
    for copy in kv_out + q_out[:5]:
        copy.start()

    for load in loads[:3]:
        load.wait()

    for copy in halos:
        copy.wait_recv()
    zero_row = jnp.zeros((1, TC + 2, SAMPLES, C), BF)
    zero_col = jnp.zeros((TR + 2, 1, SAMPLES, C), BF)

    @pl.when(r == 0)
    def _():
        xp[0:1] = zero_row

    @pl.when(r == N_ROW - 1)
    def _():
        xp[TR + 1 : TR + 2] = zero_row

    @pl.when(c == 0)
    def _():
        xp[:, 0:1] = zero_col

    @pl.when(c == N_COL - 1)
    def _():
        xp[:, TC + 1 : TC + 2] = zero_col

    cells = xp[...].astype(F32)
    conv = jnp.zeros((TILE * SAMPLES, C), F32)
    for a in (-1, 0, 1):
        for b in (-1, 0, 1):
            window = cells[1 - a : 1 - a + TR, 1 - b : 1 - b + TC]
            window = window.reshape(TILE * SAMPLES, C).astype(BF)
            conv = conv + dot_nt(window, cw[a + 1, b + 1])
    z = zz[...].astype(F32).reshape(TILE * SAMPLES, C)
    sig = jax.nn.sigmoid(z)
    grad_z = (conv * sig * (1.0 + z * (1.0 - sig))).astype(BF)
    gz_keep[...] = grad_z.astype(F32)
    placed = dot(sel_tile[...], grad_z)
    ga = dot_nt(placed.astype(BF), ow[...])
    for s in range(SAMPLES):
        for b in range(2):
            piece = ga[s * PAD : (s + 1) * PAD, b * 128 : (b + 1) * 128]
            ga_s[2 * s + b] = piece.reshape(3, 8, 128).astype(BF)

    def flat(ref, rows):
        return ref[...].astype(F32).reshape(rows, 128).astype(BF)

    def exchange(src, dst, send, recv):
        dst[c] = src[c]
        started, arrivals = [], []
        for o in range(1, N_COL):
            to, back = lax.rem(c + o, N_COL), lax.rem(c + N_COL - o, N_COL)
            started.append(push(src.at[to], dst.at[c], send.at[o], recv.at[o], (r, to)))
            arrivals.append(
                push(src.at[back], dst.at[back], send.at[o], recv.at[o], (r, back))
            )
        for copy in started:
            copy.start()
        return started, arrivals

    a_out, a_in = exchange(ga_s, do_r, a_send, a_recv)
    for copy in q_out[5:]:
        copy.start()

    def unpack(src, slot, dst, left):
        x = src[slot].astype(F32)
        if left:
            top, bottom = jnp.where(lanes, x, 0.0), jnp.where(lanes, swap(x), 0.0)
        else:
            top, bottom = jnp.where(lanes, 0.0, swap(x)), jnp.where(lanes, 0.0, x)
        top, bottom = top.astype(BF), bottom.astype(BF)
        at = pl.multiple_of(slot * PART_A, PART_A)
        dst[pl.ds(at, HALF_A)] = top[:HALF_A]
        dst[pl.ds(at + HALF_A, HALF_A)] = bottom[:HALF_A]
        at = pl.multiple_of(LEN_A + slot * PART_B, 32)
        dst[pl.ds(at, HALF_B)] = top[HALF_A:]
        dst[pl.ds(at + HALF_B, HALF_B)] = bottom[HALF_A:]

    for o in range(4):
        for copy in kv_in[o]:
            copy.wait_recv()
    keys = kv_r.reshape(BLOCK, 128)
    v_t1[:, 64:80, :] = jnp.ones((CHUNKS, 16, CHUNK), BF)
    for k in range(CHUNKS):
        turned = dot_nt(eye[...], keys[k * CHUNK : (k + 1) * CHUNK]).astype(BF)
        k_t[k] = turned[:64]
        v_t1[k, 0:64, :] = turned[64:]

    for copy in a_in:
        copy.wait_recv()
    for load in loads[3:]:
        load.wait()
    halves(dot(sel_strip[...], flat(do_r, N_COL * PAD)), opk)
    o_out, o_in = gather(opk, o_r, q_peer, q_slot, ring, (1, 3, 2), o_send, o_recv)
    for copy in o_out:
        copy.start()

    def stats_chunk(at, width):
        here = pl.ds(at, width)
        scores = dot_nt(keys[...], qz[here])
        top = jnp.max(scores, axis=0, keepdims=True) * KAPPA
        e = jnp.exp2(scores * KAPPA - top)
        st_s[0:1, here] = top
        st_s[1:2, here] = jnp.sum(e, axis=0, keepdims=True)
        eb = e.astype(BF)
        e_s[:, here] = eb
        acc = jnp.zeros((80, width), F32)
        for k in range(CHUNKS):
            acc = acc + dot(v_t1[k], eb[k * CHUNK : (k + 1) * CHUNK])
        st_s[2:3, here] = acc[64:65]
        o_t[:, here] = acc[:64]

    def stats_member(o):
        for copy in q_in[o]:
            copy.wait_recv()

        for k in range(2):
            unpack(q_r, q_slot(o) * 2 + k, qz, True)
        return o

    def stats_part(o):
        stats_chunk(pl.multiple_of(q_slot(o) * 2 * PART_A, 128), 2 * PART_A)

    for o in (0, 1, 3, 2):
        stats_part(stats_member(o))

    stats_chunk(LEN_A, LEN_B)

    def share(src, dst, send, recv):
        dst[0] = src[...]
        started, arrivals = [], []
        for o in (2, 1, 3):
            peer = (q_peer(o) + core, c)
            started.append(push(src, dst.at[ring(o)], send.at[o], recv.at[ring(o)], peer))
            arrivals.append(push(src, dst.at[o], send.at[o], recv.at[o], peer))
        for copy in started:
            copy.start()
        return started, arrivals

    lse_s[...] = st_s[0:1] + jnp.log(st_s[1:2]) * LOG2E
    l_out, l_in = share(lse_s, lse_r, l_send, l_recv)
    for o in range(4):
        for copy in o_in[o]:
            copy.wait_recv()
    for k in range(8):
        unpack(o_r, k, oz, False)
    do_t = dot_nt(eye[64:], oz[...])
    rd_s[...] = jnp.sum(o_t[...] * do_t, axis=0, keepdims=True) / st_s[2:3]
    t_out, t_in = share(rd_s, rd_r, t_send, t_recv)
    for copy in l_in:
        copy.wait_recv()
    logs = [lse_r[n] for n in range(4)]
    top = jnp.maximum(jnp.maximum(logs[0], logs[1]), jnp.maximum(logs[2], logs[3]))
    norm = sum(jnp.exp2(log - top) for log in logs)
    log_norm = top + jnp.log(norm) * LOG2E
    rescale = jnp.exp2(st_s[0:1] - log_norm)
    shares = [jnp.exp2(log - log_norm) for log in logs]
    for copy in t_in:
        copy.wait_recv()
    row_dot = sum(share * rd_r[n] for n, share in enumerate(shares))

    dq_t[...] = jnp.zeros_like(dq_t)
    mine = 6 + core

    def part_copy(k):
        at = pl.multiple_of(k * STRIP, 32)
        o = 3 - k // 2
        return push(
            kvo.at[pl.ds(at, STRIP)], kv_part.at[core, o], p_send.at[k],
            p_recv.at[core, o], (k_peer(o) + lax.rem(k, 2), c),
        )

    def grad_pass(lo, width, last):
        part = slice(lo, lo + width)

        def step(j, carry):
            at = pl.multiple_of(j * CHUNK, CHUNK)
            probs = e_s[pl.ds(at, CHUNK), part].astype(F32) * rescale[:, part]
            grad_probs = dot_nt(keys[pl.ds(at, CHUNK)], oz[part])
            grad_scores = (probs * (grad_probs - row_dot[:, part])).astype(BF)
            both = dot(grad_scores, qz[part]) + dot(probs.astype(BF), oz[part])
            dq_t[0:64, part] += dot(k_t[j], grad_scores)
            if not last:
                kv_acc[pl.ds(at, CHUNK)] = both
                return carry
            both = both + kv_acc[pl.ds(at, CHUNK)]
            kvo[pl.ds(at, CHUNK)] = jnp.where(lanes_chunk, both * FACTOR, both).astype(BF)
            k = j - 1

            @pl.when(jnp.logical_and(k >= 0, k != mine))
            def _():
                part_copy(k).start()

            return carry

        lax.fori_loop(0, CHUNKS, step, 0, unroll=3)

    def send_queries(part, half, src, dst, send, recv):
        turned = dq_t[:, part].T * FACTOR
        for k in range(8):
            first = turned[2 * k * half : (2 * k + 1) * half]
            second = turned[(2 * k + 1) * half : (2 * k + 2) * half]
            src[k] = (first + swap(second)).astype(BF)
        dst[core, 0] = src[mq * 2 + core]
        started = [
            push(src.at[q_slot(o) * 2 + p], dst.at[core, ring(o)], send.at[2 * o + p],
                 recv.at[core, ring(o)], (q_peer(o) + p, c))
            for o in (2, 1, 3) for p in range(2)
        ]
        started.append(
            push(src.at[mq * 2 + other], dst.at[core, 0], send.at[0], recv.at[core, 0],
                 (r + 1 - 2 * core, c))
        )
        for copy in started:
            copy.start()
        return started

    grad_pass(0, LEN_A, False)
    d_out = send_queries(slice(0, LEN_A), HALF_A, qa, qa_part, d_send, d_recv)
    grad_pass(LEN_A, LEN_B, True)
    kv_part[core, 0] = kvo[pl.ds(pl.multiple_of(mine * STRIP, 32), STRIP)]
    d_out += send_queries(slice(LEN_A, BLOCK), HALF_B, qb, qb_part, e_send, e_recv)

    def arrive(src, dst, send, recv, peer):
        push(src, dst.at[other, 0], send.at[0], recv.at[other, 0],
             (r + 1 - 2 * core, c)).wait_recv()
        for o in range(1, 4):
            for p in range(2):
                push(src, dst.at[p, o], send.at[0], recv.at[p, o], (peer(o) + p, c)).wait_recv()

    arrive(kvo.at[pl.ds(0, STRIP)], kv_part, p_send, p_recv, k_peer)
    kv0, kv1 = [sum(kv_part[p, n].astype(F32) for n in range(4)) for p in range(2)]
    dk = jnp.where(lanes_strip, kv0, swap(kv1)).astype(BF)
    dv = jnp.where(lanes_strip, swap(kv0), kv1).astype(BF)

    def weight(kind):
        return iw[:, pl.ds(pl.multiple_of(kind * C + lax.rem(c, 2) * 128, 128), 128)]

    def unpacked(part, keep):
        q0, q1 = [sum(part[p, n].astype(F32) for n in range(4)) for p in range(2)]
        both = [jnp.where(keep, q0, swap(q1)), jnp.where(keep, swap(q0), q1)]
        return jnp.concatenate(both, axis=0).astype(BF)

    arrive(qa.at[0], qa_part, d_send, d_recv, q_peer)
    projected = dot_nt(dk, weight(1)) + dot_nt(dv, weight(2))
    first = projected[:PART_A] + dot_nt(unpacked(qa_part, lanes[:HALF_A]), weight(0))
    projected = jnp.concatenate([first, projected[PART_A:]], axis=0).astype(BF)
    projected = jnp.concatenate([projected[:, :128], projected[:, 128:]], axis=0)
    placed = dot(sel_back[...], projected)
    g_s[...] = placed.reshape(N_COL, MSG // 8, 8, 128).astype(BF)
    b_out, b_in = exchange(g_s, g_r, b_send, b_recv)

    arrive(qb.at[0], qb_part, e_send, e_recv, q_peer)
    placed = dot(row_back[...], unpacked(qb_part, lanes[:HALF_B]))
    h_s[...] = placed.reshape(N_COL, 8, 128).astype(BF)
    h_out, h_in = exchange(h_s, h_r, h_send, h_recv)
    rows = TILE * SAMPLES
    for copy in b_in:
        copy.wait_recv()
    sums = dot(sel_got[...], flat(g_r, N_COL * MSG))
    total = gz_keep[...] + jnp.concatenate([sums[:rows], sums[rows:]], axis=1)
    for copy in h_in:
        copy.wait_recv()
    late = total[(TR - 1) * TC * SAMPLES :]
    for b in range(2):
        got = jnp.concatenate([h_r[2 * s + b].astype(F32) for s in range(SAMPLES)], axis=0)
        got = dot(row_got[...], got.astype(BF)).astype(BF)
        late = late + dot_nt(got, iw[:, b * 128 : (b + 1) * 128])
    total = jnp.concatenate([total[: (TR - 1) * TC * SAMPLES], late], axis=0)
    out[...] = total.astype(BF)

    for copy in halos + kv_out + q_out + a_out + o_out + l_out + t_out + b_out + h_out:
        copy.wait_send()
    for copy in d_out:
        copy.wait_send()
    for k in range(8):

        @pl.when(k != mine)
        def _():
            part_copy(k).wait_send()


def shards(
    pre_silu, out_grad, query_heads, key_heads, value_heads, conv_weight, out_weight, input_weight
):
    sel = [jnp.asarray(x, BF) for x in selections()]
    turn = lambda x: jnp.transpose(x, (0, 2, 1))
    og = jnp.transpose(out_grad, (1, 2, 0, 3))
    zz = jnp.transpose(pre_silu, (1, 2, 0, 3))
    vmem = pl.BlockSpec(memory_space=pltpu.VMEM)
    dma = lambda *n: pltpu.SemaphoreType.DMA(n)
    result = pl.pallas_call(
        kernel,
        out_shape=jax.ShapeDtypeStruct((TILE * SAMPLES, C), BF),
        in_specs=[vmem] * 6 + [pl.BlockSpec(memory_space=pl.ANY)] * 9,
        out_specs=vmem,
        scratch_shapes=[
            *[pltpu.VMEM(x.shape, BF) for x in (conv_weight, out_weight, input_weight, *sel)],
            dma(9),
            pltpu.VMEM((TR + 2, TC + 2, SAMPLES, C), BF),
            pltpu.VMEM((TILE * SAMPLES, C), F32),
            pltpu.VMEM((N_COL, PAD // 8, 8, 128), BF),
            pltpu.VMEM((N_COL, PAD // 8, 8, 128), BF),
            pltpu.VMEM((2, HALF, 128), BF),
            pltpu.VMEM((2, HALF, 128), BF),
            pltpu.VMEM((2, STRIP, 128), BF),
            pltpu.VMEM((8, HALF, 128), BF),
            pltpu.VMEM((8, HALF, 128), BF),
            pltpu.VMEM((8, STRIP, 128), BF),
            pltpu.VMEM((BLOCK, 128), BF),
            pltpu.VMEM((BLOCK, 128), BF),
            pltpu.VMEM((CHUNKS, 64, CHUNK), BF),
            pltpu.VMEM((CHUNKS, 80, CHUNK), BF),
            pltpu.VMEM((64, BLOCK), F32),
            pltpu.VMEM((BLOCK, BLOCK), BF),
            pltpu.VMEM((4, BLOCK), F32),
            pltpu.VMEM((1, BLOCK), F32),
            pltpu.VMEM((4, 1, BLOCK), F32),
            pltpu.VMEM((1, BLOCK), F32),
            pltpu.VMEM((4, 1, BLOCK), F32),
            pltpu.VMEM((BLOCK, 128), F32),
            pltpu.VMEM((BLOCK, 128), BF),
            pltpu.VMEM((2, 4, STRIP, 128), BF),
            pltpu.VMEM((128, BLOCK), F32),
            pltpu.VMEM((8, HALF_A, 128), BF),
            pltpu.VMEM((8, HALF_B, 128), BF),
            pltpu.VMEM((2, 4, HALF_A, 128), BF),
            pltpu.VMEM((2, 4, HALF_B, 128), BF),
            pltpu.VMEM((N_COL, MSG // 8, 8, 128), BF),
            pltpu.VMEM((N_COL, MSG // 8, 8, 128), BF),
            pltpu.VMEM((N_COL, 8, 128), BF),
            pltpu.VMEM((N_COL, 8, 128), BF),
            dma(8), dma(8), dma(16), dma(16), dma(8), dma(8), dma(8), dma(8),
            dma(8), dma(8), dma(4), dma(4), dma(4), dma(4), dma(8), dma(2, 4), dma(8), dma(2, 4),
            dma(8), dma(2, 4), dma(16), dma(16), dma(16), dma(16),
        ],
        compiler_params=pltpu.CompilerParams(
            collective_id=0, has_side_effects=True, vmem_limit_bytes=56 * 2**20
        ),
    )(
        og, zz, turn(query_heads), turn(key_heads), turn(value_heads), jnp.asarray(np.eye(128), BF),
        conv_weight, out_weight, input_weight, *sel,
    )
    return jnp.transpose(result.reshape(TR, TC, SAMPLES, C), (2, 0, 1, 3))


def solution(mesh):
    in_specs = (
        P(None, "row", "col", None),
        P(None, "row", "col", None),
        P("col", "row", None),
        P("col", "row", None),
        P("col", "row", None),
        P(),
        P(),
        P(),
    )
    out_specs = P(None, "row", "col", None)
    return jax.shard_map(shards, mesh=mesh, in_specs=in_specs, out_specs=out_specs, check_vma=False)
```

```python
import functools

import jax
import jax.numpy as jnp
import numpy as np
from jax import lax
from jax.experimental import pallas as pl
from jax.experimental.pallas import tpu as pltpu
from jax.sharding import PartitionSpec as P

BF = jnp.bfloat16
F32 = jnp.float32
SAMPLES, HEADS, HD, C = 8, 4, 64, 256
TR, TC = 3, 6
N_ROW, N_COL = 32, 16
WID = TC * N_COL
STRIP = TR * WID
HALF = STRIP // 2
BLOCK = 8 * STRIP
CHUNK = 256
CHUNKS = BLOCK // CHUNK
PAD = 24
TILE = TR * TC
MESH = pl.DeviceIdType.MESH
FACTOR = HD**-0.5
LOG2E = float(np.log2(np.e))
KAPPA = FACTOR * LOG2E
NT = (((1,), (1,)), ((), ()))


PART_A = 192
PART_B = STRIP - PART_A
HALF_A, HALF_B = PART_A // 2, PART_B // 2
LEN_A = 8 * PART_A
LEN_B = 8 * PART_B
MSG = 40


def selections():
    tile = np.zeros((SAMPLES * PAD, TILE * SAMPLES), np.float32)
    strip = np.zeros((STRIP, N_COL * PAD), np.float32)
    back = np.zeros((N_COL * MSG, 2 * STRIP), np.float32)
    got = np.zeros((2 * TILE * SAMPLES, N_COL * MSG), np.float32)
    for t in range(TILE):
        for s in range(SAMPLES):
            tile[s * PAD + t, t * SAMPLES + s] = 1.0
        for n in range(N_COL):
            place = (t // TC) * WID + n * TC + t % TC
            strip[place, n * PAD + t] = 1.0
            row = t * SAMPLES + n // 2
            for half in range(2):
                back[n * MSG + half * TILE + t, half * STRIP + place] = 1.0
                got[half * TILE * SAMPLES + row, n * MSG + half * TILE + t] = 1.0
    row_back = np.zeros((N_COL * 8, PART_B), np.float32)
    row_got = np.zeros((TC * SAMPLES, SAMPLES * 8), np.float32)
    for t in range(TC):
        for n in range(N_COL):
            row_back[n * 8 + t, n * TC + t] = 1.0
        for s in range(SAMPLES):
            row_got[t * SAMPLES + s, s * 8 + t] = 1.0
    return tile, strip, back, got, row_back, row_got


def dot(a, b):
    return jnp.dot(a, b, preferred_element_type=F32)


def dot_nt(a, b):
    return lax.dot_general(a, b, NT, preferred_element_type=F32)


def swap(x):
    return pltpu.roll(x, 64, 1)


def kernel(
    og, zz, qh, kh, vh, eye, *refs,
):
    (
        hbm_cw, hbm_ow, hbm_iw, hbm_tile, hbm_strip, hbm_back, hbm_got, hbm_row_back, hbm_row_got,
        out,
        cw, ow, iw, sel_tile, sel_strip, sel_back, sel_got, row_back, row_got, load_sem,
        xp, gz_keep, ga_s, do_r, qpk, opk, kvpk, q_r, o_r, kv_r, qz, oz, k_t, v_t1,
        o_t, e_s, st_s, lse_s, lse_r, rd_s, rd_r, kv_acc, kvo, kv_part, dq_t, qa, qb,
        qa_part, qb_part, g_s, g_r, h_s, h_r,
        halo_send, halo_recv, a_send, a_recv, q_send, q_recv, o_send, o_recv,
        k_send, k_recv, l_send, l_recv, t_send, t_recv, p_send, p_recv, d_send, d_recv,
        e_send, e_recv, b_send, b_recv, h_send, h_recv,
    ) = refs
    r = lax.axis_index("row")
    c = lax.axis_index("col")
    loads = [
        pltpu.make_async_copy(src, dst, load_sem.at[n])
        for n, (src, dst) in enumerate(
            [(hbm_cw, cw), (hbm_tile, sel_tile), (hbm_ow, ow), (hbm_strip, sel_strip),
             (hbm_iw, iw), (hbm_back, sel_back), (hbm_got, sel_got),
             (hbm_row_back, row_back), (hbm_row_got, row_got)]
        )
    ]
    core = lax.rem(r, 2)
    other = 1 - core
    zi = lax.rem(r // 2, 8)
    xh = r // 16
    zl = lax.rem(zi, 2)
    mq = zi // 2

    def q_peer(o):
        return xh * 16 + (2 * lax.rem(mq + o, 4) + zl) * 2

    def k_peer(o):
        return lax.rem(xh + o // 2, 2) * 16 + (2 * mq + lax.rem(zl + lax.rem(o, 2), 2)) * 2

    def wrap(x, n):
        return lax.rem(x + n, n)

    lanes = lax.broadcasted_iota(jnp.int32, (HALF, 128), 1) < 64
    lanes_strip = lax.broadcasted_iota(jnp.int32, (STRIP, 128), 1) < 64
    lanes_chunk = lax.broadcasted_iota(jnp.int32, (CHUNK, 128), 1) < 64

    barrier = pltpu.get_barrier_semaphore()
    shifts = [(i, j) for i in (-1, 0, 1) for j in (-1, 0, 1) if (i, j) != (0, 0)]
    peers = [(wrap(r + i, N_ROW), wrap(c + j, N_COL)) for i, j in shifts]
    peers += [(r, lax.rem(c + o, N_COL)) for o in range(2, N_COL - 1)]
    for peer in (q_peer, k_peer):
        for o in range(1, 4):
            peers += [(peer(o), c), (peer(o) + 1, c)]
    peers += [(r + 1 - 2 * core, c)]
    for peer in peers:
        pl.semaphore_signal(barrier, inc=1, device_id=peer, device_id_type=MESH)

    for load in loads:
        load.start()

    def halves(x, dst):
        top = jnp.concatenate([x[:HALF_A], x[PART_A : PART_A + HALF_B]], axis=0)
        bottom = jnp.concatenate([x[HALF_A:PART_A], x[PART_A + HALF_B :]], axis=0)
        dst[0] = jnp.where(lanes, top, swap(bottom)).astype(BF)
        dst[1] = jnp.where(lanes, swap(top), bottom).astype(BF)

    for p in range(2):
        kvpk[p] = jnp.concatenate([kh[p], vh[p]], axis=0).T
    halves(jnp.concatenate([qh[0], qh[1]], axis=0).T.astype(F32), qpk)
    xp[1:4, 1:7] = og[...]
    pl.semaphore_wait(barrier, len(peers))

    def push(src, dst, send, recv, peer):
        copy = pltpu.make_async_remote_copy(
            src_ref=src, dst_ref=dst, send_sem=send, recv_sem=recv,
            device_id=peer, device_id_type=MESH,
        )
        return copy

    def rim(shift, width, take):
        if shift == 0:
            return pl.ds(0, width) if take else pl.ds(1, width)
        if take:
            return pl.ds(width - 1, 1) if shift == 1 else pl.ds(0, 1)
        return pl.ds(0, 1) if shift == 1 else pl.ds(width + 1, 1)

    halos = []
    for index, (i, j) in enumerate(shifts):
        halos.append(
            push(
                og.at[rim(i, TR, True), rim(j, TC, True)],
                xp.at[rim(i, TR, False), rim(j, TC, False)],
                halo_send.at[index], halo_recv.at[index],
                (wrap(r + i, N_ROW), wrap(c + j, N_COL)),
            )
        )
    for copy in halos:
        copy.start()

    def gather(src, dst, peer, slot, turn, order, send, recv):
        here = (r + 1 - 2 * core, c)
        dst[slot(0) * 2 + core] = src[core]
        started = [
            push(src.at[other], dst.at[slot(0) * 2 + core], send.at[0], recv.at[0], here)
        ]
        arrivals = {
            0: [push(src.at[0], dst.at[slot(0) * 2 + other], send.at[0], recv.at[0], here)]
        }
        for o in order:
            there = turn(o)
            arrivals[o] = []
            for p in range(2):
                started.append(
                    push(src.at[p], dst.at[slot(o, True) * 2 + core], send.at[2 * o + p],
                         recv.at[2 * there + core], (peer(o) + p, c))
                )
                arrivals[o].append(
                    push(src.at[p], dst.at[slot(o) * 2 + p], send.at[2 * o + p],
                         recv.at[2 * o + p], (peer(o) + p, c))
                )
        return started, arrivals

    def k_slot(o, remote=False):
        return 3 - o

    def q_slot(o, remote=False):
        return mq if remote else lax.rem(mq + o, 4)

    ring = lambda o: (4 - o) % 4
    kv_out, kv_in = gather(kvpk, kv_r, k_peer, k_slot, lambda o: o, (1, 2, 3), k_send, k_recv)
    q_out, q_in = gather(qpk, q_r, q_peer, q_slot, ring, (1, 3, 2), q_send, q_recv)
    for copy in kv_out + q_out[:5]:
        copy.start()

    for load in loads[:3]:
        load.wait()

    for copy in halos:
        copy.wait_recv()
    zero_row = jnp.zeros((1, TC + 2, SAMPLES, C), BF)
    zero_col = jnp.zeros((TR + 2, 1, SAMPLES, C), BF)

    @pl.when(r == 0)
    def _():
        xp[0:1] = zero_row

    @pl.when(r == N_ROW - 1)
    def _():
        xp[TR + 1 : TR + 2] = zero_row

    @pl.when(c == 0)
    def _():
        xp[:, 0:1] = zero_col

    @pl.when(c == N_COL - 1)
    def _():
        xp[:, TC + 1 : TC + 2] = zero_col

    cells = xp[...].astype(F32)
    conv = jnp.zeros((TILE * SAMPLES, C), F32)
    for a in (-1, 0, 1):
        for b in (-1, 0, 1):
            window = cells[1 - a : 1 - a + TR, 1 - b : 1 - b + TC]
            window = window.reshape(TILE * SAMPLES, C).astype(BF)
            conv = conv + dot_nt(window, cw[a + 1, b + 1])
    z = zz[...].astype(F32).reshape(TILE * SAMPLES, C)
    sig = jax.nn.sigmoid(z)
    grad_z = (conv * sig * (1.0 + z * (1.0 - sig))).astype(BF)
    gz_keep[...] = grad_z.astype(F32)
    placed = dot(sel_tile[...], grad_z)
    ga = dot_nt(placed.astype(BF), ow[...])
    for s in range(SAMPLES):
        for b in range(2):
            piece = ga[s * PAD : (s + 1) * PAD, b * 128 : (b + 1) * 128]
            ga_s[2 * s + b] = piece.reshape(3, 8, 128).astype(BF)

    def flat(ref, rows):
        return ref[...].astype(F32).reshape(rows, 128).astype(BF)

    def exchange(src, dst, send, recv):
        dst[c] = src[c]
        started, arrivals = [], []
        for o in range(1, N_COL):
            to, back = lax.rem(c + o, N_COL), lax.rem(c + N_COL - o, N_COL)
            started.append(push(src.at[to], dst.at[c], send.at[o], recv.at[o], (r, to)))
            arrivals.append(
                push(src.at[back], dst.at[back], send.at[o], recv.at[o], (r, back))
            )
        for copy in started:
            copy.start()
        return started, arrivals

    a_out, a_in = exchange(ga_s, do_r, a_send, a_recv)
    for copy in q_out[5:]:
        copy.start()

    def unpack(src, slot, dst, left):
        x = src[slot].astype(F32)
        if left:
            top, bottom = jnp.where(lanes, x, 0.0), jnp.where(lanes, swap(x), 0.0)
        else:
            top, bottom = jnp.where(lanes, 0.0, swap(x)), jnp.where(lanes, 0.0, x)
        top, bottom = top.astype(BF), bottom.astype(BF)
        at = pl.multiple_of(slot * PART_A, PART_A)
        dst[pl.ds(at, HALF_A)] = top[:HALF_A]
        dst[pl.ds(at + HALF_A, HALF_A)] = bottom[:HALF_A]
        at = pl.multiple_of(LEN_A + slot * PART_B, 32)
        dst[pl.ds(at, HALF_B)] = top[HALF_A:]
        dst[pl.ds(at + HALF_B, HALF_B)] = bottom[HALF_A:]

    for o in range(4):
        for copy in kv_in[o]:
            copy.wait_recv()
    keys = kv_r.reshape(BLOCK, 128)
    v_t1[:, 64:80, :] = jnp.ones((CHUNKS, 16, CHUNK), BF)
    for k in range(CHUNKS):
        turned = dot_nt(eye[...], keys[k * CHUNK : (k + 1) * CHUNK]).astype(BF)
        k_t[k] = turned[:64]
        v_t1[k, 0:64, :] = turned[64:]

    for copy in a_in:
        copy.wait_recv()
    for load in loads[3:]:
        load.wait()
    halves(dot(sel_strip[...], flat(do_r, N_COL * PAD)), opk)
    o_out, o_in = gather(opk, o_r, q_peer, q_slot, ring, (1, 3, 2), o_send, o_recv)
    for copy in o_out:
        copy.start()

    def stats_chunk(at, width):
        here = pl.ds(at, width)
        scores = dot_nt(keys[...], qz[here])
        top = jnp.max(scores, axis=0, keepdims=True) * KAPPA
        e = jnp.exp2(scores * KAPPA - top)
        st_s[0:1, here] = top
        st_s[1:2, here] = jnp.sum(e, axis=0, keepdims=True)
        eb = e.astype(BF)
        e_s[:, here] = eb
        acc = jnp.zeros((80, width), F32)
        for k in range(CHUNKS):
            acc = acc + dot(v_t1[k], eb[k * CHUNK : (k + 1) * CHUNK])
        st_s[2:3, here] = acc[64:65]
        o_t[:, here] = acc[:64]

    def stats_member(o):
        for copy in q_in[o]:
            copy.wait_recv()

        for k in range(2):
            unpack(q_r, q_slot(o) * 2 + k, qz, True)
        return o

    def stats_part(o):
        stats_chunk(pl.multiple_of(q_slot(o) * 2 * PART_A, 128), 2 * PART_A)

    for o in (0, 1, 3, 2):
        stats_part(stats_member(o))

    def cotangents(o):
        for copy in o_in[o]:
            copy.wait_recv()
        for k in range(2):
            unpack(o_r, q_slot(o) * 2 + k, oz, False)

    for o in (0, 1, 3):
        cotangents(o)
    stats_chunk(LEN_A, LEN_B)

    def share(src, dst, send, recv):
        dst[0] = src[...]
        started, arrivals = [], []
        for o in (2, 1, 3):
            peer = (q_peer(o) + core, c)
            started.append(push(src, dst.at[ring(o)], send.at[o], recv.at[ring(o)], peer))
            arrivals.append(push(src, dst.at[o], send.at[o], recv.at[o], peer))
        for copy in started:
            copy.start()
        return started, arrivals

    lse_s[...] = st_s[0:1] + jnp.log(st_s[1:2]) * LOG2E
    l_out, l_in = share(lse_s, lse_r, l_send, l_recv)
    cotangents(2)
    do_t = dot_nt(eye[64:], oz[...])
    rd_s[...] = jnp.sum(o_t[...] * do_t, axis=0, keepdims=True) / st_s[2:3]
    t_out, t_in = share(rd_s, rd_r, t_send, t_recv)
    for copy in l_in:
        copy.wait_recv()
    logs = [lse_r[n] for n in range(4)]
    top = jnp.maximum(jnp.maximum(logs[0], logs[1]), jnp.maximum(logs[2], logs[3]))
    norm = sum(jnp.exp2(log - top) for log in logs)
    log_norm = top + jnp.log(norm) * LOG2E
    rescale = jnp.exp2(st_s[0:1] - log_norm)
    shares = [jnp.exp2(log - log_norm) for log in logs]
    for copy in t_in:
        copy.wait_recv()
    row_dot = sum(share * rd_r[n] for n, share in enumerate(shares))

    dq_t[...] = jnp.zeros_like(dq_t)
    mine = 6 + core

    def part_copy(k):
        at = pl.multiple_of(k * STRIP, 32)
        o = 3 - k // 2
        return push(
            kvo.at[pl.ds(at, STRIP)], kv_part.at[core, o], p_send.at[k],
            p_recv.at[core, o], (k_peer(o) + lax.rem(k, 2), c),
        )

    def grad_pass(lo, width, last):
        part = slice(lo, lo + width)

        def step(j, carry):
            at = pl.multiple_of(j * CHUNK, CHUNK)
            probs = e_s[pl.ds(at, CHUNK), part].astype(F32) * rescale[:, part]
            grad_probs = dot_nt(keys[pl.ds(at, CHUNK)], oz[part])
            grad_scores = (probs * (grad_probs - row_dot[:, part])).astype(BF)
            both = dot(grad_scores, qz[part]) + dot(probs.astype(BF), oz[part])
            dq_t[0:64, part] += dot(k_t[j], grad_scores)
            if not last:
                kv_acc[pl.ds(at, CHUNK)] = both
                return carry
            both = both + kv_acc[pl.ds(at, CHUNK)]
            kvo[pl.ds(at, CHUNK)] = jnp.where(lanes_chunk, both * FACTOR, both).astype(BF)
            k = j - 1

            @pl.when(jnp.logical_and(k >= 0, k != mine))
            def _():
                part_copy(k).start()

            return carry

        lax.fori_loop(0, CHUNKS, step, 0, unroll=3)

    def send_queries(part, half, src, dst, send, recv):
        turned = dq_t[:, part].T * FACTOR
        for k in range(8):
            first = turned[2 * k * half : (2 * k + 1) * half]
            second = turned[(2 * k + 1) * half : (2 * k + 2) * half]
            src[k] = (first + swap(second)).astype(BF)
        dst[core, 0] = src[mq * 2 + core]
        started = [
            push(src.at[q_slot(o) * 2 + p], dst.at[core, ring(o)], send.at[2 * o + p],
                 recv.at[core, ring(o)], (q_peer(o) + p, c))
            for o in (2, 1, 3) for p in range(2)
        ]
        started.append(
            push(src.at[mq * 2 + other], dst.at[core, 0], send.at[0], recv.at[core, 0],
                 (r + 1 - 2 * core, c))
        )
        for copy in started:
            copy.start()
        return started

    grad_pass(0, LEN_A, False)
    d_out = send_queries(slice(0, LEN_A), HALF_A, qa, qa_part, d_send, d_recv)
    grad_pass(LEN_A, LEN_B, True)
    kv_part[core, 0] = kvo[pl.ds(pl.multiple_of(mine * STRIP, 32), STRIP)]
    d_out += send_queries(slice(LEN_A, BLOCK), HALF_B, qb, qb_part, e_send, e_recv)

    def arrive(src, dst, send, recv, peer):
        push(src, dst.at[other, 0], send.at[0], recv.at[other, 0],
             (r + 1 - 2 * core, c)).wait_recv()
        for o in range(1, 4):
            for p in range(2):
                push(src, dst.at[p, o], send.at[0], recv.at[p, o], (peer(o) + p, c)).wait_recv()

    arrive(kvo.at[pl.ds(0, STRIP)], kv_part, p_send, p_recv, k_peer)
    kv0, kv1 = [sum(kv_part[p, n].astype(F32) for n in range(4)) for p in range(2)]
    dk = jnp.where(lanes_strip, kv0, swap(kv1)).astype(BF)
    dv = jnp.where(lanes_strip, swap(kv0), kv1).astype(BF)

    def weight(kind):
        return iw[:, pl.ds(pl.multiple_of(kind * C + lax.rem(c, 2) * 128, 128), 128)]

    def unpacked(part, keep):
        q0, q1 = [sum(part[p, n].astype(F32) for n in range(4)) for p in range(2)]
        both = [jnp.where(keep, q0, swap(q1)), jnp.where(keep, swap(q0), q1)]
        return jnp.concatenate(both, axis=0).astype(BF)

    arrive(qa.at[0], qa_part, d_send, d_recv, q_peer)
    projected = dot_nt(dk, weight(1)) + dot_nt(dv, weight(2))
    first = projected[:PART_A] + dot_nt(unpacked(qa_part, lanes[:HALF_A]), weight(0))
    projected = jnp.concatenate([first, projected[PART_A:]], axis=0).astype(BF)
    projected = jnp.concatenate([projected[:, :128], projected[:, 128:]], axis=0)
    placed = dot(sel_back[...], projected)
    g_s[...] = placed.reshape(N_COL, MSG // 8, 8, 128).astype(BF)
    b_out, b_in = exchange(g_s, g_r, b_send, b_recv)

    arrive(qb.at[0], qb_part, e_send, e_recv, q_peer)
    placed = dot(row_back[...], unpacked(qb_part, lanes[:HALF_B]))
    h_s[...] = placed.reshape(N_COL, 8, 128).astype(BF)
    h_out, h_in = exchange(h_s, h_r, h_send, h_recv)
    rows = TILE * SAMPLES
    for copy in b_in:
        copy.wait_recv()
    sums = dot(sel_got[...], flat(g_r, N_COL * MSG))
    total = gz_keep[...] + jnp.concatenate([sums[:rows], sums[rows:]], axis=1)
    for copy in h_in:
        copy.wait_recv()
    late = total[(TR - 1) * TC * SAMPLES :]
    for b in range(2):
        got = jnp.concatenate([h_r[2 * s + b].astype(F32) for s in range(SAMPLES)], axis=0)
        got = dot(row_got[...], got.astype(BF)).astype(BF)
        late = late + dot_nt(got, iw[:, b * 128 : (b + 1) * 128])
    total = jnp.concatenate([total[: (TR - 1) * TC * SAMPLES], late], axis=0)
    out[...] = total.astype(BF)

    for copy in halos + kv_out + q_out + a_out + o_out + l_out + t_out + b_out + h_out:
        copy.wait_send()
    for copy in d_out:
        copy.wait_send()
    for k in range(8):

        @pl.when(k != mine)
        def _():
            part_copy(k).wait_send()


def shards(
    pre_silu, out_grad, query_heads, key_heads, value_heads, conv_weight, out_weight, input_weight
):
    sel = [jnp.asarray(x, BF) for x in selections()]
    turn = lambda x: jnp.transpose(x, (0, 2, 1))
    og = jnp.transpose(out_grad, (1, 2, 0, 3))
    zz = jnp.transpose(pre_silu, (1, 2, 0, 3))
    vmem = pl.BlockSpec(memory_space=pltpu.VMEM)
    dma = lambda *n: pltpu.SemaphoreType.DMA(n)
    result = pl.pallas_call(
        kernel,
        out_shape=jax.ShapeDtypeStruct((TILE * SAMPLES, C), BF),
        in_specs=[vmem] * 6 + [pl.BlockSpec(memory_space=pl.ANY)] * 9,
        out_specs=vmem,
        scratch_shapes=[
            *[pltpu.VMEM(x.shape, BF) for x in (conv_weight, out_weight, input_weight, *sel)],
            dma(9),
            pltpu.VMEM((TR + 2, TC + 2, SAMPLES, C), BF),
            pltpu.VMEM((TILE * SAMPLES, C), F32),
            pltpu.VMEM((N_COL, PAD // 8, 8, 128), BF),
            pltpu.VMEM((N_COL, PAD // 8, 8, 128), BF),
            pltpu.VMEM((2, HALF, 128), BF),
            pltpu.VMEM((2, HALF, 128), BF),
            pltpu.VMEM((2, STRIP, 128), BF),
            pltpu.VMEM((8, HALF, 128), BF),
            pltpu.VMEM((8, HALF, 128), BF),
            pltpu.VMEM((8, STRIP, 128), BF),
            pltpu.VMEM((BLOCK, 128), BF),
            pltpu.VMEM((BLOCK, 128), BF),
            pltpu.VMEM((CHUNKS, 64, CHUNK), BF),
            pltpu.VMEM((CHUNKS, 80, CHUNK), BF),
            pltpu.VMEM((64, BLOCK), F32),
            pltpu.VMEM((BLOCK, BLOCK), BF),
            pltpu.VMEM((4, BLOCK), F32),
            pltpu.VMEM((1, BLOCK), F32),
            pltpu.VMEM((4, 1, BLOCK), F32),
            pltpu.VMEM((1, BLOCK), F32),
            pltpu.VMEM((4, 1, BLOCK), F32),
            pltpu.VMEM((BLOCK, 128), F32),
            pltpu.VMEM((BLOCK, 128), BF),
            pltpu.VMEM((2, 4, STRIP, 128), BF),
            pltpu.VMEM((128, BLOCK), F32),
            pltpu.VMEM((8, HALF_A, 128), BF),
            pltpu.VMEM((8, HALF_B, 128), BF),
            pltpu.VMEM((2, 4, HALF_A, 128), BF),
            pltpu.VMEM((2, 4, HALF_B, 128), BF),
            pltpu.VMEM((N_COL, MSG // 8, 8, 128), BF),
            pltpu.VMEM((N_COL, MSG // 8, 8, 128), BF),
            pltpu.VMEM((N_COL, 8, 128), BF),
            pltpu.VMEM((N_COL, 8, 128), BF),
            dma(8), dma(8), dma(16), dma(16), dma(8), dma(8), dma(8), dma(8),
            dma(8), dma(8), dma(4), dma(4), dma(4), dma(4), dma(8), dma(2, 4), dma(8), dma(2, 4),
            dma(8), dma(2, 4), dma(16), dma(16), dma(16), dma(16),
        ],
        compiler_params=pltpu.CompilerParams(
            collective_id=0, has_side_effects=True, vmem_limit_bytes=56 * 2**20
        ),
    )(
        og, zz, turn(query_heads), turn(key_heads), turn(value_heads), jnp.asarray(np.eye(128), BF),
        conv_weight, out_weight, input_weight, *sel,
    )
    return jnp.transpose(result.reshape(TR, TC, SAMPLES, C), (2, 0, 1, 3))


def solution(mesh):
    in_specs = (
        P(None, "row", "col", None),
        P(None, "row", "col", None),
        P("col", "row", None),
        P("col", "row", None),
        P("col", "row", None),
        P(),
        P(),
        P(),
    )
    out_specs = P(None, "row", "col", None)
    return jax.shard_map(shards, mesh=mesh, in_specs=in_specs, out_specs=out_specs, check_vma=False)
```
